32 devices in a mesh: theta: 16 (over z, x, core), gz: 2 (over y).
Axes of the slice: x: 2, y: 2, z: 4, core: 2. Of those that a mesh axis runs over, the one named last changes fastest.
Arguments:
- field: float32 [16, 1024, 1024], P('gz', 'theta'), parts along dimension 0, may hold values from -6 to 6
- courant: float32 [1024], replicated, may hold values from 0.2 to 0.8
Outputs:
- advanced: float32 [16, 1024, 1024], P('gz', 'theta'), parts along dimension 0
The draws below stay inside these ranges and needn't reach their ends.
There are 2 independent parts, one for each index of `gz`. The reference program is written for one: setup_inputs(seed, part) draws one part's arguments, and reference() takes and returns one part's arrays. A program takes and returns all parts, laid end to end along the dimension named above; an argument that names none is the same for every part. Nothing has to cross between parts.
All inputs are finite; a program needn't handle non-finite values.
Results may differ from the reference program's by a relative error of at most 0.00007.
Values sent between devices are 32-bit elements; how exact they have to be, the bound alone decides.
A program may use at most 128 MiB of HBM per device.

```python
import math
import jax
import jax.numpy as jnp
from jax import lax

NR = 1024
H = 8
NTH = 1024


def shard_levels(key, dims, shards, least, high):
    gain, own = 1.0, jax.random.fold_in(key, 6)
    for axis_at, blocks in shards:
        steps = jnp.exp(jax.random.uniform(jax.random.fold_in(own, axis_at), (blocks,), jnp.float32, least / len(shards), high / len(shards)))
        gain = gain * jnp.repeat(steps, dims[axis_at] // blocks).reshape([-1 if axis == axis_at else 1 for axis in range(len(dims))])
    return gain


def noise(own_key, dims, deviation, most, split=(), kind=jnp.bfloat16):
    factor_of = shard_levels(own_key, dims, split, -0.22, 0.18) if split else 1.0
    entries = jax.random.normal(own_key, dims, jnp.float32) * deviation * factor_of
    return jnp.minimum(jnp.maximum(entries, -most), most).astype(kind)


def setup_inputs(seed: int = 0, part: int = 0) -> dict:
    streams_of = jax.random.split(jax.random.key(seed), 3)
    own_keys = jax.random.split(jax.random.fold_in(streams_of[2], part), 3)
    return {
        "field": noise(own_keys[0], (H, NTH, NR), 1.0, 6.0, ((1, 16),), jnp.float32),
        "courant": jnp.clip(jnp.exp(jax.random.uniform(streams_of[1], (NR,), jnp.float32, math.log(0.2), math.log(0.8))), 0.2, 0.8),
    }


stencil_weights = (4.0 / 5.0, -1.0 / 5.0, 4.0 / 105.0, -1.0 / 280.0)
radial_step = 0.2


def diameter_blocks(radial_count):
    intervals = 2 * radial_count - 1
    row_index = jnp.arange(radial_count, dtype=jnp.int32)[:, None]
    col_index = jnp.arange(2 * radial_count, dtype=jnp.int32)[None, :]
    angle_unit = math.pi / (2 * intervals)
    summed = (row_index + col_index).astype(jnp.float32) * angle_unit
    differ = (row_index - col_index).astype(jnp.float32) * angle_unit
    spacing = -2.0 * jnp.sin(summed) * jnp.sin(differ)
    same = row_index == col_index
    row_factor = jnp.where(row_index == 0, 2.0, 1.0).astype(jnp.float32)
    col_factor = jnp.where((col_index == 0) | (col_index == intervals), 2.0, 1.0).astype(jnp.float32)
    parity = jnp.where((row_index + col_index) % 2 == 0, 1.0, -1.0).astype(jnp.float32)
    safe_spacing = jnp.where(same, 1.0, spacing)
    offdiag = jnp.where(same, 0.0, row_factor / col_factor * parity / safe_spacing)
    matrix = offdiag - jnp.where(same, jnp.sum(offdiag, axis=1, keepdims=True), 0.0)
    near = matrix[:, :radial_count].T
    far = matrix[:, radial_count:][:, ::-1].T
    return near, far


def radial_weight(radial_count):
    intervals = 2 * radial_count - 1
    angles = jnp.arange(radial_count, dtype=jnp.int32).astype(jnp.float32) * (math.pi / intervals)
    return jnp.sin(angles) ** 2


def azimuth_difference(extended, rows):
    total = jnp.zeros((extended.shape[0], rows, extended.shape[2]), jnp.float32)
    for offset in range(1, 5):
        total = total + stencil_weights[offset - 1] * (extended[:, 4 + offset:4 + offset + rows] - extended[:, 4 - offset:4 - offset + rows])
    return total


def reference(field, courant):
    near, far = diameter_blocks(NR)
    weight = radial_weight(NR)
    tau = radial_step / (2 * NR - 1)

    def section_rate(state):
        padded = jnp.concatenate([state[:, -4:], state, state[:, :4]], axis=1)
        azimuth = azimuth_difference(padded, NTH)
        opposite = jnp.roll(state, NTH // 2, axis=1)
        deriv = jnp.dot(state.reshape(-1, NR), near, precision=lax.Precision.HIGHEST) + jnp.dot(opposite.reshape(-1, NR), far, precision=lax.Precision.HIGHEST)
        deriv = deriv.reshape(state.shape)
        return -courant * azimuth - tau * weight * state * deriv

    first = field + section_rate(field)
    second = 0.75 * field + 0.25 * (first + section_rate(first))
    return field / 3.0 + (2.0 / 3.0) * (second + section_rate(second))
```

```python
import functools
import math

import jax
import jax.numpy as jnp
import numpy as np
from jax import lax
from jax.experimental import pallas as pl
from jax.experimental.pallas import tpu as pltpu
from jax.sharding import PartitionSpec as P

stencil_weights = (4.0 / 5.0, -1.0 / 5.0, 4.0 / 105.0, -1.0 / 280.0)
radial_step = 0.2
BLOCK = 256
LANES = 128
FAR = 16
HALO = 4
GROUP = 8
MESH = pl.DeviceIdType.MESH
f32, bf16 = jnp.float32, jnp.bfloat16


def best_shifts(delta, count):
    a, g, c = [1.0], [delta], [math.sqrt(1.0 - delta * delta)]
    for _ in range(9):
        a.append((a[-1] + g[-1]) / 2)
        c.append((a[-2] - g[-1]) / 2)
        g.append(math.sqrt(a[-2] * g[-1]))
    quarter = math.pi / (2 * a[-1])
    shifts = []
    for i in range(count):
        phi = 2 ** (len(a) - 1) * a[-1] * (2 * i + 1) * quarter / (2 * count)
        for k in range(len(a) - 1, 0, -1):
            phi = 0.5 * (phi + math.asin(max(-1.0, min(1.0, c[k] / a[k] * math.sin(phi)))))
        shifts.append(math.sqrt(math.cos(phi) ** 2 + (delta * math.sin(phi)) ** 2))
    return shifts


def rational_terms(points, shifts):
    columns, product = [], np.ones_like(points)
    for p in shifts:
        columns.append(math.sqrt(2 * p) / (points + p) * product)
        product = product * (points - p) / (points + p)
    return np.stack(columns, axis=1)


def rank_for(delta, tolerance):
    return math.ceil(math.log(4 / tolerance) * math.log(4 / delta) / math.pi**2)


def split_head(m):
    head = m.astype(np.float32).astype(bf16)
    tail = (m - head.astype(np.float64)).astype(np.float32).astype(bf16)
    return head, tail


def radial_tables(radial_count):
    last = 2 * radial_count - 1
    i = np.arange(radial_count)
    l = np.arange(last + 1)
    unit = np.pi / (2 * last)
    x = np.cos(2 * unit * i)
    gap = -2.0 * np.sin(unit * (i[:, None] + l)) * np.sin(unit * (i[:, None] - l))
    same = i[:, None] == l
    ci = np.where(i == 0, 2.0, 1.0)
    cl = np.where((l == 0) | (l == last), 2.0, 1.0)
    sign = np.where((i[:, None] + l) % 2 == 0, 1.0, -1.0)
    off = np.where(same, 0.0, ci[:, None] / cl * sign / np.where(same, 1.0, gap))
    near = (off - np.where(same, off.sum(axis=1)[:, None], 0.0))[:, :radial_count].T
    scale = radial_step / last * np.sin(2 * unit * i) ** 2
    blocks = radial_count // BLOCK
    diag = np.stack(
        [(near * scale)[b * BLOCK : (b + 1) * BLOCK, b * BLOCK : (b + 1) * BLOCK] for b in range(blocks)]
    )
    alternate = np.where(i % 2 == 0, 1.0, -1.0)
    row, column = alternate / ci, alternate * ci * scale
    into = np.zeros((radial_count, LANES))
    back = np.zeros((LANES, radial_count))
    at = 0
    for b in range(blocks):
        first, final = b * BLOCK, (b + 1) * BLOCK - 1
        low, high = x[final], x[first]
        above = x[first - 1] if b > 0 else x[-1]
        below = x[final + 1] if b < blocks - 1 else x[0]
        ratio = -((high - above) * (below - low)) / ((high - low) * (below - above))
        delta = ratio / (ratio + 2 + 2 * math.sqrt(ratio + 1))
        turn = (delta - 1) / (delta + 1) * (high - below) / (high - low)
        under = (x - below) - turn * (x - low)
        mapped = ((x - below) + turn * (x - low)) / under
        det = 2 * turn * (low - below)
        inside = (i >= first) & (i <= final)
        count = rank_for(delta, 1e-10)
        shifts = best_shifts(delta, count)
        into[inside, at : at + count] = rational_terms(mapped[inside], shifts) / under[inside, None]
        outer = rational_terms(-mapped[~inside], shifts) / under[~inside, None]
        back[at : at + count, ~inside] = (-det * outer).T
        at += count
    assert at <= LANES - FAR
    far = rational_terms(x, best_shifts(x[-1], FAR))
    into[:, LANES - FAR :] = far
    back[LANES - FAR :] = -far.T
    into *= row[:, None]
    back *= column
    diag_parts = np.stack(split_head(diag))
    into_parts = np.concatenate(split_head(into), axis=1)
    back_head, back_tail = split_head(back)
    back_parts = np.stack(
        [np.concatenate([back_head, back_head]), np.concatenate([back_tail, back_tail])]
    )
    return diag_parts, into_parts, back_parts


def kernel(
    size,
    field,
    courant_in,
    diag_in,
    into_in,
    back_in,
    out,
    courant,
    diag,
    into,
    back,
    raw,
    state,
    head,
    tail,
    coef,
    pair,
    deriv,
    packed,
    inbox,
    load_sem,
    table_sem,
    halo_send,
    halo_recv,
    coef_send,
    coef_recv,
):
    heights, rows, radial_count = field.shape
    blocks = radial_count // BLOCK
    groups = rows // GROUP
    rest = groups - 1
    span = GROUP * heights
    inner = rest * span
    tiles = radial_count // LANES
    me = lax.axis_index("theta")
    right = lax.rem(me + 1, size)
    left = lax.rem(me + size - 1, size)
    across = lax.rem(me + size // 2, size)

    barrier = pltpu.get_barrier_semaphore()
    for d in (right, left, across):
        pl.semaphore_signal(barrier, inc=1, device_id={"theta": d}, device_id_type=MESH)

    loads = [
        pltpu.make_async_copy(
            field.at[h, :, pl.ds(t * LANES, LANES)], raw.at[t, pl.ds(h * rows, rows)], load_sem.at[t, h]
        )
        for t in range(tiles)
        for h in range(heights)
    ]
    pairs = ((courant_in, courant), (into_in, into), (diag_in, diag), (back_in, back))
    tables = [pltpu.make_async_copy(a, b, table_sem.at[k]) for k, (a, b) in enumerate(pairs)]
    for copy in loads + tables:
        copy.start()

    def halo(sec, way):
        if way == 0:
            source, target, device = HALO + rows - HALO, 0, right
        else:
            source, target, device = HALO, HALO + rows, left
        return pltpu.make_async_remote_copy(
            state.at[sec, pl.ds(source, HALO)],
            state.at[sec, pl.ds(target, HALO)],
            halo_send.at[sec, way],
            halo_recv.at[sec, way],
            device_id={"theta": device},
            device_id_type=MESH,
        )

    def coefs(sec, part):
        where = pl.ds(0, 1) if part == 0 else pl.ds(1, rest)
        return pltpu.make_async_remote_copy(
            packed.at[sec, where],
            inbox.at[sec, where],
            coef_send.at[sec, part],
            coef_recv.at[sec, part],
            device_id={"theta": across},
            device_id_type=MESH,
        )

    def keep_split(value, at, cols):
        value = value.reshape(-1, value.shape[-1])
        top = value.astype(bf16)
        head[pl.ds(at, value.shape[0]), cols] = top
        tail[pl.ds(at, value.shape[0]), cols] = (value - top.astype(f32)).astype(bf16)

    def place(g):
        return HALO + HALO + (g - 1) * GROUP

    lane = lax.broadcasted_iota(jnp.int32, (heights, LANES), 1)
    own = lane < LANES - FAR

    def project(at, count, sec, first_group, group_count):
        both = jnp.dot(head[pl.ds(at, count)], into[...], preferred_element_type=f32) + jnp.dot(
            tail[pl.ds(at, count)], into[...], preferred_element_type=f32
        )
        total = both[:, :LANES] + both[:, LANES:]
        coef[pl.ds(at, count)] = total
        for g in range(group_count):
            pack = jnp.zeros((heights, LANES), f32)
            for k in range(GROUP):
                r = g * span + k * heights
                moved = pltpu.roll(total[r : r + heights], (FAR * (k + 1)) % LANES, 1)
                pack = jnp.where((lane >= FAR * k) & (lane < FAR * (k + 1)), moved, pack)
            packed[sec, first_group + g] = pack

    def merge(sec, first_group, group_count):
        for g in range(first_group, first_group + group_count):
            pack = inbox[sec, g]
            mixed = []
            for k in range(GROUP):
                r = g * span + k * heights
                moved = pltpu.roll(pack, (LANES - FAR * (k + 1)) % LANES, 1)
                mixed.append(jnp.where(own, coef[r : r + heights], moved))
            mixed = jnp.concatenate(mixed, axis=0)
            top = mixed.astype(bf16)
            pair[pl.ds(g * span, span), 0:LANES] = top
            pair[pl.ds(g * span, span), LANES : 2 * LANES] = (mixed - top.astype(f32)).astype(bf16)

    def differentiate(at, count):
        where = pl.ds(at, count)

        @pl.loop(0, blocks)
        def _(b):
            cols = pl.ds(pl.multiple_of(b * BLOCK, BLOCK), BLOCK)
            top = head[where, cols]
            both = pair[where]
            deriv[where, cols] = (
                jnp.dot(top, diag[0, b], preferred_element_type=f32)
                + jnp.dot(tail[where, cols], diag[0, b], preferred_element_type=f32)
                + jnp.dot(top, diag[1, b], preferred_element_type=f32)
                + jnp.dot(both, back[0, :, cols], preferred_element_type=f32)
                + jnp.dot(both, back[1, :, cols], preferred_element_type=f32)
            )

    def update(sec, first, count, at):
        start_part = (0.0, 0.75, 1.0 / 3.0)[sec]
        step_part = (1.0, 0.25, 2.0 / 3.0)[sec]
        for t in range(tiles):
            cols = slice(t * LANES, (t + 1) * LANES)
            speed = jnp.broadcast_to(courant[:, cols], (heights, LANES))
            x = state[sec, pl.ds(first - HALO, count + 2 * HALO), :, cols]
            now = x[HALO : HALO + count]
            azimuth = None
            for o in range(1, 5):
                term = stencil_weights[o - 1] * (x[HALO + o : HALO + o + count] - x[HALO - o : HALO - o + count])
                azimuth = term if azimuth is None else azimuth + term
            slope = deriv[pl.ds(at, count * heights), cols].reshape(count, heights, LANES)
            moved = now - speed * azimuth - now * slope
            if sec > 0:
                moved = start_part * state[0, pl.ds(first, count), :, cols] + step_part * moved
            if sec < 2:
                state[sec + 1, pl.ds(first, count), :, cols] = moved
                keep_split(moved, at, cols)
            else:
                raw[t, pl.ds((first - HALO) * heights, count * heights)] = moved.reshape(-1, LANES)

    def emit(g):
        for t in range(tiles):
            for h in range(heights):
                out[pl.ds(pl.multiple_of(h * rows + g * GROUP, GROUP), GROUP), t * LANES : (t + 1) * LANES] = raw[
                    t, pl.ds(g * span + h, GROUP, stride=heights)
                ]

    for copy in loads:
        copy.wait()

    def stage(first, count, at):
        for t in range(tiles):
            cols = slice(t * LANES, (t + 1) * LANES)
            value = jnp.stack([raw[t, pl.ds(first - HALO + k, heights, stride=rows)] for k in range(count)])
            state[0, pl.ds(first, count), :, cols] = value
            keep_split(value, at, cols)

    stage(HALO, HALO, 0)
    stage(rows, HALO, HALO * heights)

    @pl.loop(1, groups)
    def _(g):
        stage(place(g), GROUP, pl.multiple_of(g * span, span))

    pl.semaphore_wait(barrier, 3)
    halo(0, 0).start()
    halo(0, 1).start()
    for copy in tables:
        copy.wait()
    project(0, span, 0, 0, 1)
    coefs(0, 0).start()
    project(span, inner, 0, 1, rest)
    coefs(0, 1).start()

    for sec in range(3):
        coefs(sec, 1).wait_recv()
        merge(sec, 1, rest)
        differentiate(span, inner)

        @pl.loop(1, groups)
        def _(g):
            update(sec, place(g), GROUP, pl.multiple_of(g * span, span))

        if sec < 2:
            project(span, inner, sec + 1, 1, rest)
            coefs(sec + 1, 1).start()
        else:

            @pl.loop(1, groups - 1)
            def _(g):
                emit(g)

        coefs(sec, 0).wait_recv()
        merge(sec, 0, 1)
        differentiate(0, span)
        halo(sec, 0).wait_recv()
        halo(sec, 1).wait_recv()
        update(sec, HALO, HALO, 0)
        update(sec, rows, HALO, HALO * heights)
        if sec < 2:
            halo(sec + 1, 0).start()
            halo(sec + 1, 1).start()
            project(0, span, sec + 1, 0, 1)
            coefs(sec + 1, 0).start()
    emit(0)
    emit(groups - 1)

    for sec in range(3):
        for k in range(2):
            halo(sec, k).wait_send()
            coefs(sec, k).wait_send()


def body(size, field, courant):
    heights, rows, radial_count = field.shape
    tables = [jnp.asarray(t) for t in radial_tables(radial_count)]
    groups = rows // GROUP
    dma = pltpu.SemaphoreType.DMA
    anywhere = pl.BlockSpec(memory_space=pl.ANY)
    operands = [field, courant.reshape(1, -1)] + tables
    result = pl.pallas_call(
        functools.partial(kernel, size),
        out_shape=pltpu.VMEM((heights * rows, radial_count), f32),
        in_specs=[anywhere] * len(operands),
        out_specs=pl.BlockSpec(memory_space=pltpu.VMEM),
        scratch_shapes=[
            pltpu.VMEM((1, radial_count), f32),
            *[pltpu.VMEM(t.shape, bf16) for t in tables],
            pltpu.VMEM((radial_count // LANES, heights * rows, LANES), f32),
            pltpu.VMEM((3, rows + 2 * HALO, heights, radial_count), f32),
            pltpu.VMEM((rows * heights, radial_count), bf16),
            pltpu.VMEM((rows * heights, radial_count), bf16),
            pltpu.VMEM((rows * heights, LANES), f32),
            pltpu.VMEM((rows * heights, 2 * LANES), bf16),
            pltpu.VMEM((rows * heights, radial_count), f32),
            pltpu.VMEM((3, groups, heights, LANES), f32),
            pltpu.VMEM((3, groups, heights, LANES), f32),
            dma((radial_count // LANES, heights)),
            dma((4,)),
            dma((3, 2)),
            dma((3, 2)),
            dma((3, 2)),
            dma((3, 2)),
        ],
        compiler_params=pltpu.CompilerParams(
            collective_id=0, has_side_effects=True, vmem_limit_bytes=40 << 20
        ),
    )(*[pltpu.with_memory_space_constraint(x, pltpu.HBM) for x in operands])
    return result.reshape(field.shape)


def solution(mesh):
    size = mesh.shape["theta"]
    return jax.shard_map(
        functools.partial(body, size),
        mesh=mesh,
        in_specs=(P("gz", "theta", None), P()),
        out_specs=P("gz", "theta", None),
        check_vma=False,
    )
```

```python
import functools
import math

import jax
import jax.numpy as jnp
import numpy as np
from jax import lax
from jax.experimental import pallas as pl
from jax.experimental.pallas import tpu as pltpu
from jax.sharding import PartitionSpec as P

stencil_weights = (4.0 / 5.0, -1.0 / 5.0, 4.0 / 105.0, -1.0 / 280.0)
radial_step = 0.2
BLOCK = 256
LANES = 128
FAR = 16
HALO = 4
GROUP = 8
MESH = pl.DeviceIdType.MESH
f32, bf16 = jnp.float32, jnp.bfloat16
fills = (
    (0, 0, BLOCK),
    (0, BLOCK, BLOCK),
    (BLOCK, 2 * BLOCK, BLOCK),
    (2 * BLOCK, 3 * BLOCK, LANES),
    (2 * BLOCK, 3 * BLOCK + LANES, LANES),
    (2 * BLOCK + LANES, 4 * BLOCK, LANES),
    (2 * BLOCK + LANES, 4 * BLOCK + LANES, LANES),
)


def best_shifts(delta, count):
    a, g, c = [1.0], [delta], [math.sqrt(1.0 - delta * delta)]
    for _ in range(9):
        a.append((a[-1] + g[-1]) / 2)
        c.append((a[-2] - g[-1]) / 2)
        g.append(math.sqrt(a[-2] * g[-1]))
    quarter = math.pi / (2 * a[-1])
    shifts = []
    for i in range(count):
        phi = 2 ** (len(a) - 1) * a[-1] * (2 * i + 1) * quarter / (2 * count)
        for k in range(len(a) - 1, 0, -1):
            phi = 0.5 * (phi + math.asin(max(-1.0, min(1.0, c[k] / a[k] * math.sin(phi)))))
        shifts.append(math.sqrt(math.cos(phi) ** 2 + (delta * math.sin(phi)) ** 2))
    return shifts


def rational_terms(points, shifts):
    columns, product = [], np.ones_like(points)
    for p in shifts:
        columns.append(math.sqrt(2 * p) / (points + p) * product)
        product = product * (points - p) / (points + p)
    return np.stack(columns, axis=1)


def rank_for(delta, tolerance):
    return math.ceil(math.log(4 / tolerance) * math.log(4 / delta) / math.pi**2)


def split_head(m):
    head = m.astype(np.float32).astype(bf16)
    tail = (m - head.astype(np.float64)).astype(np.float32).astype(bf16)
    return head, tail


def radial_tables(radial_count):
    last = 2 * radial_count - 1
    i = np.arange(radial_count)
    l = np.arange(last + 1)
    unit = np.pi / (2 * last)
    x = np.cos(2 * unit * i)
    gap = -2.0 * np.sin(unit * (i[:, None] + l)) * np.sin(unit * (i[:, None] - l))
    same = i[:, None] == l
    ci = np.where(i == 0, 2.0, 1.0)
    cl = np.where((l == 0) | (l == last), 2.0, 1.0)
    sign = np.where((i[:, None] + l) % 2 == 0, 1.0, -1.0)
    off = np.where(same, 0.0, ci[:, None] / cl * sign / np.where(same, 1.0, gap))
    near = (off - np.where(same, off.sum(axis=1)[:, None], 0.0))[:, :radial_count].T
    scale = radial_step / last * np.sin(2 * unit * i) ** 2
    blocks = radial_count // BLOCK
    diag = np.stack(
        [(near * scale)[b * BLOCK : (b + 1) * BLOCK, b * BLOCK : (b + 1) * BLOCK] for b in range(blocks)]
    )
    alternate = np.where(i % 2 == 0, 1.0, -1.0)
    row, column = alternate / ci, alternate * ci * scale
    into = np.zeros((radial_count, LANES))
    back = np.zeros((LANES, radial_count))
    at = 0
    for b in range(blocks):
        first, final = b * BLOCK, (b + 1) * BLOCK - 1
        low, high = x[final], x[first]
        above = x[first - 1] if b > 0 else x[-1]
        below = x[final + 1] if b < blocks - 1 else x[0]
        ratio = -((high - above) * (below - low)) / ((high - low) * (below - above))
        delta = ratio / (ratio + 2 + 2 * math.sqrt(ratio + 1))
        turn = (delta - 1) / (delta + 1) * (high - below) / (high - low)
        under = (x - below) - turn * (x - low)
        mapped = ((x - below) + turn * (x - low)) / under
        det = 2 * turn * (low - below)
        inside = (i >= first) & (i <= final)
        count = rank_for(delta, 1e-10)
        shifts = best_shifts(delta, count)
        into[inside, at : at + count] = rational_terms(mapped[inside], shifts) / under[inside, None]
        outer = rational_terms(-mapped[~inside], shifts) / under[~inside, None]
        back[at : at + count, ~inside] = (-det * outer).T
        at += count
    assert at <= LANES - FAR
    far = rational_terms(x, best_shifts(x[-1], FAR))
    into[:, LANES - FAR :] = far
    back[LANES - FAR :] = -far.T
    into *= row[:, None]
    back *= column
    diag_head, diag_tail = split_head(diag)
    into_parts = np.concatenate(split_head(into), axis=1)
    back_head, back_tail = split_head(back)
    back_head, back_tail = [m.reshape(LANES, blocks, BLOCK).transpose(1, 0, 2) for m in (back_head, back_tail)]
    both_parts = np.concatenate([diag_head, diag_tail, back_head, back_tail], axis=1)
    return into_parts, both_parts


def kernel(
    size,
    field,
    courant_in,
    into_in,
    both_in,
    out,
    courant,
    into,
    both,
    raw,
    state,
    head,
    tail,
    coef,
    pair,
    deriv,
    packed,
    inbox,
    load_sem,
    table_sem,
    halo_send,
    halo_recv,
    coef_send,
    coef_recv,
):
    heights, rows, radial_count = field.shape
    blocks = radial_count // BLOCK
    groups = rows // GROUP
    span = GROUP * heights
    middle = (groups + 2) // 2
    parts = ((0, 1), (1, middle), (middle, groups))
    tiles = radial_count // LANES
    me = lax.axis_index("theta")
    right = lax.rem(me + 1, size)
    left = lax.rem(me + size - 1, size)
    across = lax.rem(me + size // 2, size)

    barrier = pltpu.get_barrier_semaphore()
    for d in (right, left, across):
        pl.semaphore_signal(barrier, inc=1, device_id={"theta": d}, device_id_type=MESH)

    loads = [
        pltpu.make_async_copy(
            field.at[h, :, pl.ds(t * LANES, LANES)], raw.at[t, pl.ds(h * rows, rows)], load_sem.at[t, h]
        )
        for t in range(tiles)
        for h in range(heights)
    ]
    pairs = [(courant_in, courant), (into_in, into)]
    for source, target, count in fills:
        pairs.append((both_in.at[:, pl.ds(source, count)], both.at[:, pl.ds(target, count)]))
    tables = [pltpu.make_async_copy(a, b, table_sem.at[k]) for k, (a, b) in enumerate(pairs)]
    for copy in loads + tables:
        copy.start()

    def halo(sec, way, b):
        if way == 0:
            source, target, device = HALO + rows - HALO, 0, right
        else:
            source, target, device = HALO, HALO + rows, left
        cols = pl.ds(b * BLOCK, BLOCK)
        return pltpu.make_async_remote_copy(
            state.at[sec, pl.ds(source, HALO), :, cols],
            state.at[sec, pl.ds(target, HALO), :, cols],
            halo_send.at[sec, way, b],
            halo_recv.at[sec, way, b],
            device_id={"theta": device},
            device_id_type=MESH,
        )

    def coefs(sec, part):
        first, stop = parts[part]
        where = pl.ds(first, stop - first)
        return pltpu.make_async_remote_copy(
            packed.at[sec, where],
            inbox.at[sec, where],
            coef_send.at[sec, part],
            coef_recv.at[sec, part],
            device_id={"theta": across},
            device_id_type=MESH,
        )

    def keep_split(value, at, cols):
        value = value.reshape(-1, value.shape[-1])
        top = value.astype(bf16)
        head[pl.ds(at, value.shape[0]), cols] = top
        tail[pl.ds(at, value.shape[0]), cols] = (value - top.astype(f32)).astype(bf16)

    def place(g):
        return HALO + HALO + (g - 1) * GROUP

    lane = lax.broadcasted_iota(jnp.int32, (heights, LANES), 1)
    own = lane < LANES - FAR

    def project(sec, part):
        first, stop = parts[part]
        where = slice(first * span, stop * span)
        double = jnp.dot(head[where], into[...], preferred_element_type=f32) + jnp.dot(
            tail[where], into[...], preferred_element_type=f32
        )
        total = double[:, :LANES] + double[:, LANES:]
        coef[where] = total
        for g in range(first, stop):
            pack = jnp.zeros((heights, LANES), f32)
            for k in range(GROUP):
                r = (g - first) * span + k * heights
                moved = pltpu.roll(total[r : r + heights], (FAR * (k + 1)) % LANES, 1)
                pack = jnp.where((lane >= FAR * k) & (lane < FAR * (k + 1)), moved, pack)
            packed[sec, g] = pack
        coefs(sec, part).start()

    def differentiate(sec, part):
        first, stop = parts[part]
        coefs(sec, part).wait_recv()
        for g in range(first, stop):
            pack = inbox[sec, g]
            mixed = []
            for k in range(GROUP):
                r = g * span + k * heights
                moved = pltpu.roll(pack, (LANES - FAR * (k + 1)) % LANES, 1)
                mixed.append(jnp.where(own, coef[r : r + heights], moved))
            mixed = jnp.concatenate(mixed, axis=0)
            top = mixed.astype(bf16)
            pair[g * span : (g + 1) * span, 0:LANES] = top
            pair[g * span : (g + 1) * span, LANES : 2 * LANES] = (mixed - top.astype(f32)).astype(bf16)
        where = slice(first * span, stop * span)
        for b in range(blocks):
            cols = slice(b * BLOCK, (b + 1) * BLOCK)
            top = head[where, cols]
            far = pair[where]
            wide = jnp.concatenate([top, tail[where, cols], top, far, far], axis=1)
            deriv[where, cols] = jnp.dot(wide, both[b], preferred_element_type=f32)

    def update(sec, first, count, at, b):
        start_part = (0.0, 0.75, 1.0 / 3.0)[sec]
        step_part = (1.0, 0.25, 2.0 / 3.0)[sec]
        for t in range(b * BLOCK // LANES, (b + 1) * BLOCK // LANES):
            cols = slice(t * LANES, (t + 1) * LANES)
            speed = jnp.broadcast_to(courant[:, cols], (heights, LANES))
            x = state[sec, pl.ds(first - HALO, count + 2 * HALO), :, cols]
            now = x[HALO : HALO + count]
            azimuth = None
            for o in range(1, 5):
                term = stencil_weights[o - 1] * (x[HALO + o : HALO + o + count] - x[HALO - o : HALO - o + count])
                azimuth = term if azimuth is None else azimuth + term
            slope = deriv[pl.ds(at, count * heights), cols].reshape(count, heights, LANES)
            moved = now - speed * azimuth - now * slope
            if sec > 0:
                moved = start_part * state[0, pl.ds(first, count), :, cols] + step_part * moved
            if sec < 2:
                state[sec + 1, pl.ds(first, count), :, cols] = moved
                keep_split(moved, at, cols)
            else:
                raw[t, pl.ds((first - HALO) * heights, count * heights)] = moved.reshape(-1, LANES)

    def emit(g):
        for t in range(tiles):
            for h in range(heights):
                out[pl.ds(pl.multiple_of(h * rows + g * GROUP, GROUP), GROUP), t * LANES : (t + 1) * LANES] = raw[
                    t, pl.ds(g * span + h, GROUP, stride=heights)
                ]

    for copy in loads:
        copy.wait()

    def stage(first, count, at):
        for t in range(tiles):
            cols = slice(t * LANES, (t + 1) * LANES)
            value = jnp.stack([raw[t, pl.ds(first - HALO + k, heights, stride=rows)] for k in range(count)])
            state[0, pl.ds(first, count), :, cols] = value
            keep_split(value, at, cols)

    stage(HALO, HALO, 0)
    stage(rows, HALO, HALO * heights)

    @pl.loop(1, groups)
    def _(g):
        stage(place(g), GROUP, pl.multiple_of(g * span, span))

    def inner(sec, part):
        differentiate(sec, part)
        for b in range(blocks):
            for g in range(*parts[part]):
                update(sec, place(g), GROUP, g * span, b)
        if sec < 2:
            project(sec + 1, part)

    def edges(sec):
        differentiate(sec, 0)
        for b in range(blocks):
            halo(sec, 0, b).wait_recv()
            halo(sec, 1, b).wait_recv()
            update(sec, HALO, HALO, 0, b)
            update(sec, rows, HALO, HALO * heights, b)
            if sec < 2:
                halo(sec + 1, 0, b).start()
                halo(sec + 1, 1, b).start()
        if sec < 2:
            project(sec + 1, 0)

    pl.semaphore_wait(barrier, 3)
    for b in range(blocks):
        halo(0, 0, b).start()
        halo(0, 1, b).start()
    for copy in tables:
        copy.wait()
    for part in range(len(parts)):
        project(0, part)

    for sec in range(2):
        inner(sec, 1)
        edges(sec)
        inner(sec, 2)
    inner(2, 1)
    inner(2, 2)

    @pl.loop(1, groups - 1)
    def _(g):
        emit(g)

    edges(2)
    emit(0)
    emit(groups - 1)

    for sec in range(3):
        for way in range(2):
            for b in range(blocks):
                halo(sec, way, b).wait_send()
        for part in range(len(parts)):
            coefs(sec, part).wait_send()


def body(size, field, courant):
    heights, rows, radial_count = field.shape
    tables = [jnp.asarray(t) for t in radial_tables(radial_count)]
    groups = rows // GROUP
    dma = pltpu.SemaphoreType.DMA
    anywhere = pl.BlockSpec(memory_space=pl.ANY)
    operands = [field, courant.reshape(1, -1)] + tables
    result = pl.pallas_call(
        functools.partial(kernel, size),
        out_shape=pltpu.VMEM((heights * rows, radial_count), f32),
        in_specs=[anywhere] * len(operands),
        out_specs=pl.BlockSpec(memory_space=pltpu.VMEM),
        scratch_shapes=[
            pltpu.VMEM((1, radial_count), f32),
            pltpu.VMEM(tables[0].shape, bf16),
            pltpu.VMEM((radial_count // BLOCK, 5 * BLOCK, BLOCK), bf16),
            pltpu.VMEM((radial_count // LANES, heights * rows, LANES), f32),
            pltpu.VMEM((3, rows + 2 * HALO, heights, radial_count), f32),
            pltpu.VMEM((rows * heights, radial_count), bf16),
            pltpu.VMEM((rows * heights, radial_count), bf16),
            pltpu.VMEM((rows * heights, LANES), f32),
            pltpu.VMEM((rows * heights, 2 * LANES), bf16),
            pltpu.VMEM((rows * heights, radial_count), f32),
            pltpu.VMEM((3, groups, heights, LANES), f32),
            pltpu.VMEM((3, groups, heights, LANES), f32),
            dma((radial_count // LANES, heights)),
            dma((2 + len(fills),)),
            dma((3, 2, radial_count // BLOCK)),
            dma((3, 2, radial_count // BLOCK)),
            dma((3, 3)),
            dma((3, 3)),
        ],
        compiler_params=pltpu.CompilerParams(
            collective_id=0, has_side_effects=True, vmem_limit_bytes=40 << 20
        ),
    )(*[pltpu.with_memory_space_constraint(x, pltpu.HBM) for x in operands])
    return result.reshape(field.shape)


def solution(mesh):
    size = mesh.shape["theta"]
    return jax.shard_map(
        functools.partial(body, size),
        mesh=mesh,
        in_specs=(P("gz", "theta", None), P()),
        out_specs=P("gz", "theta", None),
        check_vma=False,
    )
```

```python
import functools
import math

import jax
import jax.numpy as jnp
import numpy as np
from jax import lax
from jax.experimental import pallas as pl
from jax.experimental.pallas import tpu as pltpu
from jax.sharding import PartitionSpec as P

stencil_weights = (4.0 / 5.0, -1.0 / 5.0, 4.0 / 105.0, -1.0 / 280.0)
radial_step = 0.2
BLOCK = 256
LANES = 128
FAR = 16
HALO = 4
GROUP = 8
MESH = pl.DeviceIdType.MESH
f32, bf16 = jnp.float32, jnp.bfloat16
fills = (
    (0, 0, BLOCK),
    (0, BLOCK, BLOCK),
    (BLOCK, 2 * BLOCK, BLOCK),
    (2 * BLOCK, 3 * BLOCK, LANES),
    (2 * BLOCK, 3 * BLOCK + LANES, LANES),
    (2 * BLOCK + LANES, 4 * BLOCK, LANES),
    (2 * BLOCK + LANES, 4 * BLOCK + LANES, LANES),
)


def best_shifts(delta, count):
    a, g, c = [1.0], [delta], [math.sqrt(1.0 - delta * delta)]
    for _ in range(9):
        a.append((a[-1] + g[-1]) / 2)
        c.append((a[-2] - g[-1]) / 2)
        g.append(math.sqrt(a[-2] * g[-1]))
    quarter = math.pi / (2 * a[-1])
    shifts = []
    for i in range(count):
        phi = 2 ** (len(a) - 1) * a[-1] * (2 * i + 1) * quarter / (2 * count)
        for k in range(len(a) - 1, 0, -1):
            phi = 0.5 * (phi + math.asin(max(-1.0, min(1.0, c[k] / a[k] * math.sin(phi)))))
        shifts.append(math.sqrt(math.cos(phi) ** 2 + (delta * math.sin(phi)) ** 2))
    return shifts


def rational_terms(points, shifts):
    columns, product = [], np.ones_like(points)
    for p in shifts:
        columns.append(math.sqrt(2 * p) / (points + p) * product)
        product = product * (points - p) / (points + p)
    return np.stack(columns, axis=1)


def rank_for(delta, tolerance):
    return math.ceil(math.log(4 / tolerance) * math.log(4 / delta) / math.pi**2)


def split_head(m):
    head = m.astype(np.float32).astype(bf16)
    tail = (m - head.astype(np.float64)).astype(np.float32).astype(bf16)
    return head, tail


def radial_tables(radial_count):
    last = 2 * radial_count - 1
    i = np.arange(radial_count)
    l = np.arange(last + 1)
    unit = np.pi / (2 * last)
    x = np.cos(2 * unit * i)
    gap = -2.0 * np.sin(unit * (i[:, None] + l)) * np.sin(unit * (i[:, None] - l))
    same = i[:, None] == l
    ci = np.where(i == 0, 2.0, 1.0)
    cl = np.where((l == 0) | (l == last), 2.0, 1.0)
    sign = np.where((i[:, None] + l) % 2 == 0, 1.0, -1.0)
    off = np.where(same, 0.0, ci[:, None] / cl * sign / np.where(same, 1.0, gap))
    near = (off - np.where(same, off.sum(axis=1)[:, None], 0.0))[:, :radial_count].T
    scale = radial_step / last * np.sin(2 * unit * i) ** 2
    blocks = radial_count // BLOCK
    diag = np.stack(
        [(near * scale)[b * BLOCK : (b + 1) * BLOCK, b * BLOCK : (b + 1) * BLOCK] for b in range(blocks)]
    )
    alternate = np.where(i % 2 == 0, 1.0, -1.0)
    row, column = alternate / ci, alternate * ci * scale
    into = np.zeros((radial_count, LANES))
    back = np.zeros((LANES, radial_count))
    at = 0
    for b in range(blocks):
        first, final = b * BLOCK, (b + 1) * BLOCK - 1
        low, high = x[final], x[first]
        above = x[first - 1] if b > 0 else x[-1]
        below = x[final + 1] if b < blocks - 1 else x[0]
        ratio = -((high - above) * (below - low)) / ((high - low) * (below - above))
        delta = ratio / (ratio + 2 + 2 * math.sqrt(ratio + 1))
        turn = (delta - 1) / (delta + 1) * (high - below) / (high - low)
        under = (x - below) - turn * (x - low)
        mapped = ((x - below) + turn * (x - low)) / under
        det = 2 * turn * (low - below)
        inside = (i >= first) & (i <= final)
        count = rank_for(delta, 1e-10)
        shifts = best_shifts(delta, count)
        into[inside, at : at + count] = rational_terms(mapped[inside], shifts) / under[inside, None]
        outer = rational_terms(-mapped[~inside], shifts) / under[~inside, None]
        back[at : at + count, ~inside] = (-det * outer).T
        at += count
    assert at <= LANES - FAR
    far = rational_terms(x, best_shifts(x[-1], FAR))
    into[:, LANES - FAR :] = far
    back[LANES - FAR :] = -far.T
    into *= row[:, None]
    back *= column
    diag_head, diag_tail = split_head(diag)
    into_parts = np.concatenate(split_head(into), axis=1)
    back_head, back_tail = split_head(back)
    back_head, back_tail = [m.reshape(LANES, blocks, BLOCK).transpose(1, 0, 2) for m in (back_head, back_tail)]
    both_parts = np.concatenate([diag_head, diag_tail, back_head, back_tail], axis=1)
    return into_parts, both_parts


def kernel(
    size,
    field,
    courant_in,
    into_in,
    both_in,
    out,
    courant,
    into,
    both,
    raw,
    state,
    head,
    tail,
    coef,
    pair,
    deriv,
    packed,
    inbox,
    load_sem,
    table_sem,
    halo_send,
    halo_recv,
    coef_send,
    coef_recv,
):
    heights, rows, radial_count = field.shape
    blocks = radial_count // BLOCK
    groups = rows // GROUP
    span = GROUP * heights
    middle = (groups + 2) // 2
    parts = ((0, 1), (1, middle), (middle, groups))
    tiles = radial_count // LANES
    me = lax.axis_index("theta")
    right = lax.rem(me + 1, size)
    left = lax.rem(me + size - 1, size)
    across = lax.rem(me + size // 2, size)

    barrier = pltpu.get_barrier_semaphore()
    for d in (right, left, across):
        pl.semaphore_signal(barrier, inc=1, device_id={"theta": d}, device_id_type=MESH)

    loads = [
        pltpu.make_async_copy(
            field.at[h, :, pl.ds(t * LANES, LANES)], raw.at[t, pl.ds(h * rows, rows)], load_sem.at[t, h]
        )
        for t in range(tiles)
        for h in range(heights)
    ]
    pairs = [(courant_in, courant), (into_in, into)]
    for source, target, count in fills:
        pairs.append((both_in.at[:, pl.ds(source, count)], both.at[:, pl.ds(target, count)]))
    tables = [pltpu.make_async_copy(a, b, table_sem.at[k]) for k, (a, b) in enumerate(pairs)]
    for copy in loads + tables:
        copy.start()

    def halo(sec, way, b):
        if way == 0:
            source, target, device = HALO + rows - HALO, 0, right
        else:
            source, target, device = HALO, HALO + rows, left
        cols = pl.ds(b * BLOCK, BLOCK)
        return pltpu.make_async_remote_copy(
            state.at[sec, pl.ds(source, HALO), :, cols],
            state.at[sec, pl.ds(target, HALO), :, cols],
            halo_send.at[sec, way, b],
            halo_recv.at[sec, way, b],
            device_id={"theta": device},
            device_id_type=MESH,
        )

    def coefs(sec, part):
        first, stop = parts[part]
        where = pl.ds(first, stop - first)
        return pltpu.make_async_remote_copy(
            packed.at[sec, where],
            inbox.at[sec, where],
            coef_send.at[sec, part],
            coef_recv.at[sec, part],
            device_id={"theta": across},
            device_id_type=MESH,
        )

    def keep_split(value, at, cols):
        value = value.reshape(-1, value.shape[-1])
        top = value.astype(bf16)
        head[pl.ds(at, value.shape[0]), cols] = top
        tail[pl.ds(at, value.shape[0]), cols] = (value - top.astype(f32)).astype(bf16)

    def place(g):
        return HALO + HALO + (g - 1) * GROUP

    lane = lax.broadcasted_iota(jnp.int32, (heights, LANES), 1)
    own = lane < LANES - FAR

    def project(sec, part):
        first, stop = parts[part]
        where = slice(first * span, stop * span)
        double = jnp.dot(head[where], into[...], preferred_element_type=f32) + jnp.dot(
            tail[where], into[...], preferred_element_type=f32
        )
        total = double[:, :LANES] + double[:, LANES:]
        coef[where] = total
        for g in range(first, stop):
            pack = jnp.zeros((heights, LANES), f32)
            for k in range(GROUP):
                r = (g - first) * span + k * heights
                moved = pltpu.roll(total[r : r + heights], (FAR * (k + 1)) % LANES, 1)
                pack = jnp.where((lane >= FAR * k) & (lane < FAR * (k + 1)), moved, pack)
            packed[sec, g] = pack

    def differentiate(sec, part):
        first, stop = parts[part]
        coefs(sec, part).wait_recv()
        for g in range(first, stop):
            pack = inbox[sec, g]
            mixed = []
            for k in range(GROUP):
                r = g * span + k * heights
                moved = pltpu.roll(pack, (LANES - FAR * (k + 1)) % LANES, 1)
                mixed.append(jnp.where(own, coef[r : r + heights], moved))
            mixed = jnp.concatenate(mixed, axis=0)
            top = mixed.astype(bf16)
            pair[g * span : (g + 1) * span, 0:LANES] = top
            pair[g * span : (g + 1) * span, LANES : 2 * LANES] = (mixed - top.astype(f32)).astype(bf16)
        where = slice(first * span, stop * span)
        for b in range(blocks):
            cols = slice(b * BLOCK, (b + 1) * BLOCK)
            top = head[where, cols]
            far = pair[where]
            wide = jnp.concatenate([top, tail[where, cols], top, far, far], axis=1)
            deriv[where, cols] = jnp.dot(wide, both[b], preferred_element_type=f32)

    def update(sec, first, count, at, b):
        start_part = (0.0, 0.75, 1.0 / 3.0)[sec]
        step_part = (1.0, 0.25, 2.0 / 3.0)[sec]
        for t in range(b * BLOCK // LANES, (b + 1) * BLOCK // LANES):
            cols = slice(t * LANES, (t + 1) * LANES)
            speed = jnp.broadcast_to(courant[:, cols], (heights, LANES))
            x = state[sec, pl.ds(first - HALO, count + 2 * HALO), :, cols]
            now = x[HALO : HALO + count]
            azimuth = None
            for o in range(1, 5):
                term = stencil_weights[o - 1] * (x[HALO + o : HALO + o + count] - x[HALO - o : HALO - o + count])
                azimuth = term if azimuth is None else azimuth + term
            slope = deriv[pl.ds(at, count * heights), cols].reshape(count, heights, LANES)
            moved = now - speed * azimuth - now * slope
            if sec > 0:
                moved = start_part * state[0, pl.ds(first, count), :, cols] + step_part * moved
            if sec < 2:
                state[sec + 1, pl.ds(first, count), :, cols] = moved
                keep_split(moved, at, cols)
            else:
                raw[t, pl.ds((first - HALO) * heights, count * heights)] = moved.reshape(-1, LANES)

    def emit(g):
        for t in range(tiles):
            for h in range(heights):
                out[pl.ds(pl.multiple_of(h * rows + g * GROUP, GROUP), GROUP), t * LANES : (t + 1) * LANES] = raw[
                    t, pl.ds(g * span + h, GROUP, stride=heights)
                ]

    for copy in loads:
        copy.wait()

    def stage(first, count, at):
        for t in range(tiles):
            cols = slice(t * LANES, (t + 1) * LANES)
            value = jnp.stack([raw[t, pl.ds(first - HALO + k, heights, stride=rows)] for k in range(count)])
            state[0, pl.ds(first, count), :, cols] = value
            keep_split(value, at, cols)

    stage(HALO, HALO, 0)
    stage(rows, HALO, HALO * heights)

    @pl.loop(1, groups)
    def _(g):
        stage(place(g), GROUP, pl.multiple_of(g * span, span))

    def inner(sec, part):
        differentiate(sec, part)
        for b in range(blocks):
            for g in range(*parts[part]):
                update(sec, place(g), GROUP, g * span, b)
        if sec < 2:
            project(sec + 1, part)
            coefs(sec + 1, part).start()

    def edges(sec):
        differentiate(sec, 0)
        for b in range(blocks):
            halo(sec, 0, b).wait_recv()
            halo(sec, 1, b).wait_recv()
            update(sec, HALO, HALO, 0, b)
            update(sec, rows, HALO, HALO * heights, b)
            if sec < 2:
                halo(sec + 1, 0, b).start()
                halo(sec + 1, 1, b).start()
        if sec < 2:
            project(sec + 1, 0)
            coefs(sec + 1, 0).start()

    for copy in tables:
        copy.wait()
    for part in (1, 2, 0):
        project(0, part)
    pl.semaphore_wait(barrier, 3)
    for part in (1, 2, 0):
        coefs(0, part).start()
    for b in range(blocks):
        halo(0, 0, b).start()
        halo(0, 1, b).start()

    inner(0, 1)
    inner(0, 2)
    edges(0)
    inner(1, 1)
    inner(1, 2)
    edges(1)

    inner(2, 1)
    inner(2, 2)

    @pl.loop(1, groups - 1)
    def _(g):
        emit(g)

    edges(2)
    emit(0)
    emit(groups - 1)

    for sec in range(3):
        for way in range(2):
            for b in range(blocks):
                halo(sec, way, b).wait_send()
        for part in range(len(parts)):
            coefs(sec, part).wait_send()


def body(size, field, courant):
    heights, rows, radial_count = field.shape
    tables = [jnp.asarray(t) for t in radial_tables(radial_count)]
    groups = rows // GROUP
    dma = pltpu.SemaphoreType.DMA
    anywhere = pl.BlockSpec(memory_space=pl.ANY)
    operands = [field, courant.reshape(1, -1)] + tables
    result = pl.pallas_call(
        functools.partial(kernel, size),
        out_shape=pltpu.VMEM((heights * rows, radial_count), f32),
        in_specs=[anywhere] * len(operands),
        out_specs=pl.BlockSpec(memory_space=pltpu.VMEM),
        scratch_shapes=[
            pltpu.VMEM((1, radial_count), f32),
            pltpu.VMEM(tables[0].shape, bf16),
            pltpu.VMEM((radial_count // BLOCK, 5 * BLOCK, BLOCK), bf16),
            pltpu.VMEM((radial_count // LANES, heights * rows, LANES), f32),
            pltpu.VMEM((3, rows + 2 * HALO, heights, radial_count), f32),
            pltpu.VMEM((rows * heights, radial_count), bf16),
            pltpu.VMEM((rows * heights, radial_count), bf16),
            pltpu.VMEM((rows * heights, LANES), f32),
            pltpu.VMEM((rows * heights, 2 * LANES), bf16),
            pltpu.VMEM((rows * heights, radial_count), f32),
            pltpu.VMEM((3, groups, heights, LANES), f32),
            pltpu.VMEM((3, groups, heights, LANES), f32),
            dma((radial_count // LANES, heights)),
            dma((2 + len(fills),)),
            dma((3, 2, radial_count // BLOCK)),
            dma((3, 2, radial_count // BLOCK)),
            dma((3, 3)),
            dma((3, 3)),
        ],
        compiler_params=pltpu.CompilerParams(
            collective_id=0, has_side_effects=True, vmem_limit_bytes=40 << 20
        ),
    )(*[pltpu.with_memory_space_constraint(x, pltpu.HBM) for x in operands])
    return result.reshape(field.shape)


def solution(mesh):
    size = mesh.shape["theta"]
    return jax.shard_map(
        functools.partial(body, size),
        mesh=mesh,
        in_specs=(P("gz", "theta", None), P()),
        out_specs=P("gz", "theta", None),
        check_vma=False,
    )
```

```python
import functools
import math

import jax
import jax.numpy as jnp
import numpy as np
from jax import lax
from jax.experimental import pallas as pl
from jax.experimental.pallas import tpu as pltpu
from jax.sharding import PartitionSpec as P

stencil_weights = (4.0 / 5.0, -1.0 / 5.0, 4.0 / 105.0, -1.0 / 280.0)
radial_step = 0.2
BLOCK = 256
LANES = 128
FAR = 16
HALO = 4
GROUP = 8
MESH = pl.DeviceIdType.MESH
f32, bf16 = jnp.float32, jnp.bfloat16
fills = (
    (0, 0, BLOCK),
    (0, BLOCK, BLOCK),
    (BLOCK, 2 * BLOCK, BLOCK),
    (2 * BLOCK, 3 * BLOCK, LANES),
    (2 * BLOCK, 3 * BLOCK + LANES, LANES),
    (2 * BLOCK + LANES, 4 * BLOCK, LANES),
    (2 * BLOCK + LANES, 4 * BLOCK + LANES, LANES),
)


def best_shifts(delta, count):
    a, g, c = [1.0], [delta], [math.sqrt(1.0 - delta * delta)]
    for _ in range(9):
        a.append((a[-1] + g[-1]) / 2)
        c.append((a[-2] - g[-1]) / 2)
        g.append(math.sqrt(a[-2] * g[-1]))
    quarter = math.pi / (2 * a[-1])
    shifts = []
    for i in range(count):
        phi = 2 ** (len(a) - 1) * a[-1] * (2 * i + 1) * quarter / (2 * count)
        for k in range(len(a) - 1, 0, -1):
            phi = 0.5 * (phi + math.asin(max(-1.0, min(1.0, c[k] / a[k] * math.sin(phi)))))
        shifts.append(math.sqrt(math.cos(phi) ** 2 + (delta * math.sin(phi)) ** 2))
    return shifts


def rational_terms(points, shifts):
    columns, product = [], np.ones_like(points)
    for p in shifts:
        columns.append(math.sqrt(2 * p) / (points + p) * product)
        product = product * (points - p) / (points + p)
    return np.stack(columns, axis=1)


def rank_for(delta, tolerance):
    return math.ceil(math.log(4 / tolerance) * math.log(4 / delta) / math.pi**2)


def split_head(m):
    head = m.astype(np.float32).astype(bf16)
    tail = (m - head.astype(np.float64)).astype(np.float32).astype(bf16)
    return head, tail


def radial_tables(radial_count):
    last = 2 * radial_count - 1
    i = np.arange(radial_count)
    l = np.arange(last + 1)
    unit = np.pi / (2 * last)
    x = np.cos(2 * unit * i)
    gap = -2.0 * np.sin(unit * (i[:, None] + l)) * np.sin(unit * (i[:, None] - l))
    same = i[:, None] == l
    ci = np.where(i == 0, 2.0, 1.0)
    cl = np.where((l == 0) | (l == last), 2.0, 1.0)
    sign = np.where((i[:, None] + l) % 2 == 0, 1.0, -1.0)
    off = np.where(same, 0.0, ci[:, None] / cl * sign / np.where(same, 1.0, gap))
    near = (off - np.where(same, off.sum(axis=1)[:, None], 0.0))[:, :radial_count].T
    scale = radial_step / last * np.sin(2 * unit * i) ** 2
    blocks = radial_count // BLOCK
    diag = np.stack(
        [(near * scale)[b * BLOCK : (b + 1) * BLOCK, b * BLOCK : (b + 1) * BLOCK] for b in range(blocks)]
    )
    alternate = np.where(i % 2 == 0, 1.0, -1.0)
    row, column = alternate / ci, alternate * ci * scale
    into = np.zeros((radial_count, LANES))
    back = np.zeros((LANES, radial_count))
    at = 0
    for b in range(blocks):
        first, final = b * BLOCK, (b + 1) * BLOCK - 1
        low, high = x[final], x[first]
        above = x[first - 1] if b > 0 else x[-1]
        below = x[final + 1] if b < blocks - 1 else x[0]
        ratio = -((high - above) * (below - low)) / ((high - low) * (below - above))
        delta = ratio / (ratio + 2 + 2 * math.sqrt(ratio + 1))
        turn = (delta - 1) / (delta + 1) * (high - below) / (high - low)
        under = (x - below) - turn * (x - low)
        mapped = ((x - below) + turn * (x - low)) / under
        det = 2 * turn * (low - below)
        inside = (i >= first) & (i <= final)
        count = rank_for(delta, 1e-10)
        shifts = best_shifts(delta, count)
        into[inside, at : at + count] = rational_terms(mapped[inside], shifts) / under[inside, None]
        outer = rational_terms(-mapped[~inside], shifts) / under[~inside, None]
        back[at : at + count, ~inside] = (-det * outer).T
        at += count
    assert at <= LANES - FAR
    far = rational_terms(x, best_shifts(x[-1], FAR))
    into[:, LANES - FAR :] = far
    back[LANES - FAR :] = -far.T
    into *= row[:, None]
    back *= column
    diag_head, diag_tail = split_head(diag)
    into_parts = np.concatenate(split_head(into), axis=1)
    back_head, back_tail = split_head(back)
    back_head, back_tail = [m.reshape(LANES, blocks, BLOCK).transpose(1, 0, 2) for m in (back_head, back_tail)]
    both_parts = np.concatenate([diag_head, diag_tail, back_head, back_tail], axis=1)
    head, tail = back_head[:, LANES - FAR :], back_tail[:, LANES - FAR :]
    far_parts = np.concatenate([head, head, tail, tail], axis=1)
    far_parts = np.concatenate([far_parts, np.zeros((blocks, LANES - 4 * FAR, BLOCK), far_parts.dtype)], axis=1)
    return into_parts, both_parts, far_parts


def kernel(
    size,
    field,
    courant_in,
    into_in,
    both_in,
    across_in,
    out,
    courant,
    into,
    both,
    across_back,
    raw,
    state,
    head,
    tail,
    away,
    pair,
    deriv,
    packed,
    inbox,
    load_sem,
    table_sem,
    halo_send,
    halo_recv,
    coef_send,
    coef_recv,
):
    heights, rows, radial_count = field.shape
    blocks = radial_count // BLOCK
    groups = rows // GROUP
    span = GROUP * heights
    middle = (groups + 2) // 2
    parts = ((0, 1), (1, middle), (middle, groups))
    tiles = radial_count // LANES
    me = lax.axis_index("theta")
    right = lax.rem(me + 1, size)
    left = lax.rem(me + size - 1, size)
    across = lax.rem(me + size // 2, size)

    barrier = pltpu.get_barrier_semaphore()
    for d in (right, left, across):
        pl.semaphore_signal(barrier, inc=1, device_id={"theta": d}, device_id_type=MESH)

    loads = [
        pltpu.make_async_copy(
            field.at[h, :, pl.ds(t * LANES, LANES)], raw.at[t, pl.ds(h * rows, rows)], load_sem.at[t, h]
        )
        for t in range(tiles)
        for h in range(heights)
    ]
    pairs = [(courant_in, courant), (into_in, into), (across_in, across_back)]
    for source, target, count in fills:
        pairs.append((both_in.at[:, pl.ds(source, count)], both.at[:, pl.ds(target, count)]))
    tables = [pltpu.make_async_copy(a, b, table_sem.at[k]) for k, (a, b) in enumerate(pairs)]
    for copy in loads + tables:
        copy.start()

    def halo(sec, way, b):
        if way == 0:
            source, target, device = HALO + rows - HALO, 0, right
        else:
            source, target, device = HALO, HALO + rows, left
        cols = pl.ds(b * BLOCK, BLOCK)
        return pltpu.make_async_remote_copy(
            state.at[sec, pl.ds(source, HALO), :, cols],
            state.at[sec, pl.ds(target, HALO), :, cols],
            halo_send.at[sec, way, b],
            halo_recv.at[sec, way, b],
            device_id={"theta": device},
            device_id_type=MESH,
        )

    def coefs(sec, part):
        first, stop = parts[part]
        where = pl.ds(first, stop - first)
        return pltpu.make_async_remote_copy(
            packed.at[sec, where],
            inbox.at[sec, where],
            coef_send.at[sec, part],
            coef_recv.at[sec, part],
            device_id={"theta": across},
            device_id_type=MESH,
        )

    def keep_split(value, at, cols):
        value = value.reshape(-1, value.shape[-1])
        top = value.astype(bf16)
        head[pl.ds(at, value.shape[0]), cols] = top
        tail[pl.ds(at, value.shape[0]), cols] = (value - top.astype(f32)).astype(bf16)

    def place(g):
        return HALO + HALO + (g - 1) * GROUP

    lane = lax.broadcasted_iota(jnp.int32, (heights, LANES), 1)

    def project(sec, part):
        first, stop = parts[part]
        where = slice(first * span, stop * span)
        double = jnp.dot(head[where], into[...], preferred_element_type=f32) + jnp.dot(
            tail[where], into[...], preferred_element_type=f32
        )
        total = double[:, :LANES] + double[:, LANES:]
        kept = jnp.where(lax.broadcasted_iota(jnp.int32, total.shape, 1) < LANES - FAR, total, 0.0)
        top = kept.astype(bf16)
        pair[where, 0:LANES] = top
        pair[where, LANES : 2 * LANES] = (kept - top.astype(f32)).astype(bf16)
        for g in range(first, stop):
            pack = jnp.zeros((heights, LANES), f32)
            for k in range(GROUP):
                r = (g - first) * span + k * heights
                moved = pltpu.roll(total[r : r + heights], (FAR * (k + 1)) % LANES, 1)
                pack = jnp.where((lane >= FAR * k) & (lane < FAR * (k + 1)), moved, pack)
            packed[sec, g] = pack

    def near(part):
        first, stop = parts[part]
        where = slice(first * span, stop * span)
        for b in range(blocks):
            cols = slice(b * BLOCK, (b + 1) * BLOCK)
            top = head[where, cols]
            wide = jnp.concatenate([top, tail[where, cols], top, pair[where], pair[where]], axis=1)
            deriv[where, cols] = jnp.dot(wide, both[b], preferred_element_type=f32)

    def far(sec, part):
        first, stop = parts[part]
        coefs(sec, part).wait_recv()
        for g in range(first, stop):
            pack = inbox[sec, g]
            top = pack.astype(bf16).astype(f32)
            rest = pack - top
            lines = []
            for k in range(GROUP):
                line = jnp.zeros((heights, LANES), f32)
                for n in range(4):
                    moved = pltpu.roll(rest if n % 2 else top, (FAR * (n - k)) % LANES, 1)
                    line = jnp.where((lane >= FAR * n) & (lane < FAR * (n + 1)), moved, line)
                lines.append(line)
            away[g * span : (g + 1) * span] = jnp.concatenate(lines, axis=0).astype(bf16)
        where = slice(first * span, stop * span)
        for b in range(blocks):
            cols = slice(b * BLOCK, (b + 1) * BLOCK)
            deriv[where, cols] = deriv[where, cols] + jnp.dot(
                away[where], across_back[b], preferred_element_type=f32
            )

    def update(sec, first, count, at, b):
        start_part = (0.0, 0.75, 1.0 / 3.0)[sec]
        step_part = (1.0, 0.25, 2.0 / 3.0)[sec]
        for t in range(b * BLOCK // LANES, (b + 1) * BLOCK // LANES):
            cols = slice(t * LANES, (t + 1) * LANES)
            speed = jnp.broadcast_to(courant[:, cols], (heights, LANES))
            x = state[sec, pl.ds(first - HALO, count + 2 * HALO), :, cols]
            now = x[HALO : HALO + count]
            azimuth = None
            for o in range(1, 5):
                term = stencil_weights[o - 1] * (x[HALO + o : HALO + o + count] - x[HALO - o : HALO - o + count])
                azimuth = term if azimuth is None else azimuth + term
            slope = deriv[pl.ds(at, count * heights), cols].reshape(count, heights, LANES)
            moved = now - speed * azimuth - now * slope
            if sec > 0:
                moved = start_part * state[0, pl.ds(first, count), :, cols] + step_part * moved
            if sec < 2:
                state[sec + 1, pl.ds(first, count), :, cols] = moved
                keep_split(moved, at, cols)
            else:
                raw[t, pl.ds((first - HALO) * heights, count * heights)] = moved.reshape(-1, LANES)

    def emit(g):
        for t in range(tiles):
            for h in range(heights):
                out[pl.ds(pl.multiple_of(h * rows + g * GROUP, GROUP), GROUP), t * LANES : (t + 1) * LANES] = raw[
                    t, pl.ds(g * span + h, GROUP, stride=heights)
                ]

    for copy in loads:
        copy.wait()

    def stage(first, count, at):
        for t in range(tiles):
            cols = slice(t * LANES, (t + 1) * LANES)
            value = jnp.stack([raw[t, pl.ds(first - HALO + k, heights, stride=rows)] for k in range(count)])
            state[0, pl.ds(first, count), :, cols] = value
            keep_split(value, at, cols)

    stage(HALO, HALO, 0)
    stage(rows, HALO, HALO * heights)

    @pl.loop(1, groups)
    def _(g):
        stage(place(g), GROUP, pl.multiple_of(g * span, span))

    def inner(sec, part):
        far(sec, part)
        for b in range(blocks):
            for g in range(*parts[part]):
                update(sec, place(g), GROUP, g * span, b)
        if sec < 2:
            project(sec + 1, part)
            coefs(sec + 1, part).start()

    def edges(sec):
        far(sec, 0)
        for b in range(blocks):
            halo(sec, 0, b).wait_recv()
            halo(sec, 1, b).wait_recv()
            update(sec, HALO, HALO, 0, b)
            update(sec, rows, HALO, HALO * heights, b)
            if sec < 2:
                halo(sec + 1, 0, b).start()
                halo(sec + 1, 1, b).start()
        if sec < 2:
            project(sec + 1, 0)
            coefs(sec + 1, 0).start()

    for copy in tables:
        copy.wait()
    for part in (1, 2, 0):
        project(0, part)
    pl.semaphore_wait(barrier, 3)
    for part in (1, 2, 0):
        coefs(0, part).start()
    for b in range(blocks):
        halo(0, 0, b).start()
        halo(0, 1, b).start()

    for part in (1, 2, 0):
        near(part)
    for sec in range(2):
        inner(sec, 1)
        inner(sec, 2)
        near(1)
        edges(sec)
        near(2)
        near(0)
    inner(2, 1)
    inner(2, 2)

    @pl.loop(1, groups - 1)
    def _(g):
        emit(g)

    edges(2)
    emit(0)
    emit(groups - 1)

    for sec in range(3):
        for way in range(2):
            for b in range(blocks):
                halo(sec, way, b).wait_send()
        for part in range(len(parts)):
            coefs(sec, part).wait_send()


def body(size, field, courant):
    heights, rows, radial_count = field.shape
    tables = [jnp.asarray(t) for t in radial_tables(radial_count)]
    groups = rows // GROUP
    dma = pltpu.SemaphoreType.DMA
    anywhere = pl.BlockSpec(memory_space=pl.ANY)
    operands = [field, courant.reshape(1, -1)] + tables
    result = pl.pallas_call(
        functools.partial(kernel, size),
        out_shape=pltpu.VMEM((heights * rows, radial_count), f32),
        in_specs=[anywhere] * len(operands),
        out_specs=pl.BlockSpec(memory_space=pltpu.VMEM),
        scratch_shapes=[
            pltpu.VMEM((1, radial_count), f32),
            pltpu.VMEM(tables[0].shape, bf16),
            pltpu.VMEM((radial_count // BLOCK, 5 * BLOCK, BLOCK), bf16),
            pltpu.VMEM(tables[2].shape, bf16),
            pltpu.VMEM((radial_count // LANES, heights * rows, LANES), f32),
            pltpu.VMEM((3, rows + 2 * HALO, heights, radial_count), f32),
            pltpu.VMEM((rows * heights, radial_count), bf16),
            pltpu.VMEM((rows * heights, radial_count), bf16),
            pltpu.VMEM((rows * heights, LANES), bf16),
            pltpu.VMEM((rows * heights, 2 * LANES), bf16),
            pltpu.VMEM((rows * heights, radial_count), f32),
            pltpu.VMEM((3, groups, heights, LANES), f32),
            pltpu.VMEM((3, groups, heights, LANES), f32),
            dma((radial_count // LANES, heights)),
            dma((3 + len(fills),)),
            dma((3, 2, radial_count // BLOCK)),
            dma((3, 2, radial_count // BLOCK)),
            dma((3, 3)),
            dma((3, 3)),
        ],
        compiler_params=pltpu.CompilerParams(
            collective_id=0, has_side_effects=True, vmem_limit_bytes=40 << 20
        ),
    )(*[pltpu.with_memory_space_constraint(x, pltpu.HBM) for x in operands])
    return result.reshape(field.shape)


def solution(mesh):
    size = mesh.shape["theta"]
    return jax.shard_map(
        functools.partial(body, size),
        mesh=mesh,
        in_specs=(P("gz", "theta", None), P()),
        out_specs=P("gz", "theta", None),
        check_vma=False,
    )
```

```python
import functools
import math

import jax
import jax.numpy as jnp
import numpy as np
from jax import lax
from jax.experimental import pallas as pl
from jax.experimental.pallas import tpu as pltpu
from jax.sharding import PartitionSpec as P

stencil_weights = (4.0 / 5.0, -1.0 / 5.0, 4.0 / 105.0, -1.0 / 280.0)
radial_step = 0.2
BLOCK = 256
LANES = 128
FAR = 16
HALO = 4
GROUP = 8
MESH = pl.DeviceIdType.MESH
f32, bf16 = jnp.float32, jnp.bfloat16
fills = (
    (0, 0, BLOCK),
    (0, BLOCK, BLOCK),
    (BLOCK, 2 * BLOCK, BLOCK),
    (2 * BLOCK, 3 * BLOCK, LANES),
    (2 * BLOCK, 3 * BLOCK + LANES, LANES),
    (2 * BLOCK + LANES, 4 * BLOCK, LANES),
    (2 * BLOCK + LANES, 4 * BLOCK + LANES, LANES),
)


def best_shifts(delta, count):
    a, g, c = [1.0], [delta], [math.sqrt(1.0 - delta * delta)]
    for _ in range(9):
        a.append((a[-1] + g[-1]) / 2)
        c.append((a[-2] - g[-1]) / 2)
        g.append(math.sqrt(a[-2] * g[-1]))
    quarter = math.pi / (2 * a[-1])
    shifts = []
    for i in range(count):
        phi = 2 ** (len(a) - 1) * a[-1] * (2 * i + 1) * quarter / (2 * count)
        for k in range(len(a) - 1, 0, -1):
            phi = 0.5 * (phi + math.asin(max(-1.0, min(1.0, c[k] / a[k] * math.sin(phi)))))
        shifts.append(math.sqrt(math.cos(phi) ** 2 + (delta * math.sin(phi)) ** 2))
    return shifts


def rational_terms(points, shifts):
    columns, product = [], np.ones_like(points)
    for p in shifts:
        columns.append(math.sqrt(2 * p) / (points + p) * product)
        product = product * (points - p) / (points + p)
    return np.stack(columns, axis=1)


def rank_for(delta, tolerance):
    return math.ceil(math.log(4 / tolerance) * math.log(4 / delta) / math.pi**2)


def split_head(m):
    head = m.astype(np.float32).astype(bf16)
    tail = (m - head.astype(np.float64)).astype(np.float32).astype(bf16)
    return head, tail


def radial_tables(radial_count):
    last = 2 * radial_count - 1
    i = np.arange(radial_count)
    l = np.arange(last + 1)
    unit = np.pi / (2 * last)
    x = np.cos(2 * unit * i)
    gap = -2.0 * np.sin(unit * (i[:, None] + l)) * np.sin(unit * (i[:, None] - l))
    same = i[:, None] == l
    ci = np.where(i == 0, 2.0, 1.0)
    cl = np.where((l == 0) | (l == last), 2.0, 1.0)
    sign = np.where((i[:, None] + l) % 2 == 0, 1.0, -1.0)
    off = np.where(same, 0.0, ci[:, None] / cl * sign / np.where(same, 1.0, gap))
    near = (off - np.where(same, off.sum(axis=1)[:, None], 0.0))[:, :radial_count].T
    scale = radial_step / last * np.sin(2 * unit * i) ** 2
    blocks = radial_count // BLOCK
    diag = np.stack(
        [(near * scale)[b * BLOCK : (b + 1) * BLOCK, b * BLOCK : (b + 1) * BLOCK] for b in range(blocks)]
    )
    alternate = np.where(i % 2 == 0, 1.0, -1.0)
    row, column = alternate / ci, alternate * ci * scale
    into = np.zeros((radial_count, LANES))
    back = np.zeros((LANES, radial_count))
    at = 0
    for b in range(blocks):
        first, final = b * BLOCK, (b + 1) * BLOCK - 1
        low, high = x[final], x[first]
        above = x[first - 1] if b > 0 else x[-1]
        below = x[final + 1] if b < blocks - 1 else x[0]
        ratio = -((high - above) * (below - low)) / ((high - low) * (below - above))
        delta = ratio / (ratio + 2 + 2 * math.sqrt(ratio + 1))
        turn = (delta - 1) / (delta + 1) * (high - below) / (high - low)
        under = (x - below) - turn * (x - low)
        mapped = ((x - below) + turn * (x - low)) / under
        det = 2 * turn * (low - below)
        inside = (i >= first) & (i <= final)
        count = rank_for(delta, 1e-10)
        shifts = best_shifts(delta, count)
        into[inside, at : at + count] = rational_terms(mapped[inside], shifts) / under[inside, None]
        outer = rational_terms(-mapped[~inside], shifts) / under[~inside, None]
        back[at : at + count, ~inside] = (-det * outer).T
        at += count
    assert at <= LANES - FAR
    far = rational_terms(x, best_shifts(x[-1], FAR))
    into[:, LANES - FAR :] = far
    back[LANES - FAR :] = -far.T
    into *= row[:, None]
    back *= column
    diag_head, diag_tail = split_head(diag)
    into_parts = np.concatenate(split_head(into), axis=1)
    back_head, back_tail = split_head(back)
    back_head, back_tail = [m.reshape(LANES, blocks, BLOCK).transpose(1, 0, 2) for m in (back_head, back_tail)]
    both_parts = np.concatenate([diag_head, diag_tail, back_head, back_tail], axis=1)
    head, tail = back_head[:, LANES - FAR :], back_tail[:, LANES - FAR :]
    far_parts = np.concatenate([head, head, tail, tail], axis=1)
    far_parts = np.concatenate([far_parts, np.zeros((blocks, LANES - 4 * FAR, BLOCK), far_parts.dtype)], axis=1)
    return into_parts, both_parts, far_parts


def kernel(
    size,
    field,
    courant_in,
    into_in,
    both_in,
    across_in,
    out,
    courant,
    into,
    both,
    across_back,
    raw,
    state,
    head,
    tail,
    away,
    pair,
    deriv,
    packed,
    inbox,
    load_sem,
    table_sem,
    halo_send,
    halo_recv,
    coef_send,
    coef_recv,
):
    heights, rows, radial_count = field.shape
    blocks = radial_count // BLOCK
    groups = rows // GROUP
    span = GROUP * heights
    middle = (groups + 2) // 2
    parts = ((0, 1), (1, middle), (middle, groups))
    tiles = radial_count // LANES
    me = lax.axis_index("theta")
    right = lax.rem(me + 1, size)
    left = lax.rem(me + size - 1, size)
    across = lax.rem(me + size // 2, size)

    barrier = pltpu.get_barrier_semaphore()
    for d in (right, left, across):
        pl.semaphore_signal(barrier, inc=1, device_id={"theta": d}, device_id_type=MESH)

    loads = [
        pltpu.make_async_copy(
            field.at[h, :, pl.ds(t * LANES, LANES)], raw.at[t, pl.ds(h * rows, rows)], load_sem.at[t, h]
        )
        for t in range(tiles)
        for h in range(heights)
    ]
    pairs = [(courant_in, courant), (into_in, into), (across_in, across_back)]
    for source, target, count in fills:
        pairs.append((both_in.at[:, pl.ds(source, count)], both.at[:, pl.ds(target, count)]))
    tables = [pltpu.make_async_copy(a, b, table_sem.at[k]) for k, (a, b) in enumerate(pairs)]
    for copy in loads + tables:
        copy.start()

    def halo(sec, way, b):
        if way == 0:
            source, target, device = HALO + rows - HALO, 0, right
        else:
            source, target, device = HALO, HALO + rows, left
        cols = pl.ds(b * BLOCK, BLOCK)
        return pltpu.make_async_remote_copy(
            state.at[sec, pl.ds(source, HALO), :, cols],
            state.at[sec, pl.ds(target, HALO), :, cols],
            halo_send.at[sec, way, b],
            halo_recv.at[sec, way, b],
            device_id={"theta": device},
            device_id_type=MESH,
        )

    def coefs(sec, part):
        first, stop = parts[part]
        where = pl.ds(first, stop - first)
        return pltpu.make_async_remote_copy(
            packed.at[sec, where],
            inbox.at[sec, where],
            coef_send.at[sec, part],
            coef_recv.at[sec, part],
            device_id={"theta": across},
            device_id_type=MESH,
        )

    def keep_split(value, at, cols):
        value = value.reshape(-1, value.shape[-1])
        top = value.astype(bf16)
        head[pl.ds(at, value.shape[0]), cols] = top
        tail[pl.ds(at, value.shape[0]), cols] = (value - top.astype(f32)).astype(bf16)

    def place(g):
        return HALO + HALO + (g - 1) * GROUP

    lane = lax.broadcasted_iota(jnp.int32, (heights, LANES), 1)

    def project(sec, part):
        first, stop = parts[part]
        where = slice(first * span, stop * span)
        for b in range(blocks):
            cols = slice(b * BLOCK, (b + 1) * BLOCK)
            line = jnp.concatenate([head[where, cols], tail[where, cols]], axis=1)
            deriv[where, cols] = jnp.dot(
                line, jnp.concatenate([into[cols], into[cols]], axis=0), preferred_element_type=f32
            )
        total = functools.reduce(
            lambda a, b: a + b, [deriv[where, k * LANES : (k + 1) * LANES] for k in range(radial_count // LANES)]
        )
        kept = jnp.where(lax.broadcasted_iota(jnp.int32, total.shape, 1) < LANES - FAR, total, 0.0)
        top = kept.astype(bf16)
        pair[where, 0:LANES] = top
        pair[where, LANES : 2 * LANES] = (kept - top.astype(f32)).astype(bf16)
        for g in range(first, stop):
            pack = jnp.zeros((heights, LANES), f32)
            for k in range(GROUP):
                r = (g - first) * span + k * heights
                moved = pltpu.roll(total[r : r + heights], (FAR * (k + 1)) % LANES, 1)
                pack = jnp.where((lane >= FAR * k) & (lane < FAR * (k + 1)), moved, pack)
            packed[sec, g] = pack

    def near(part):
        first, stop = parts[part]
        where = slice(first * span, stop * span)
        for b in range(blocks):
            cols = slice(b * BLOCK, (b + 1) * BLOCK)
            top = head[where, cols]
            wide = jnp.concatenate([top, tail[where, cols], top, pair[where], pair[where]], axis=1)
            deriv[where, cols] = jnp.dot(wide, both[b], preferred_element_type=f32)

    def far(sec, part):
        first, stop = parts[part]
        coefs(sec, part).wait_recv()
        for g in range(first, stop):
            pack = inbox[sec, g]
            top = pack.astype(bf16).astype(f32)
            rest = pack - top
            lines = []
            for k in range(GROUP):
                line = jnp.zeros((heights, LANES), f32)
                for n in range(4):
                    moved = pltpu.roll(rest if n % 2 else top, (FAR * (n - k)) % LANES, 1)
                    line = jnp.where((lane >= FAR * n) & (lane < FAR * (n + 1)), moved, line)
                lines.append(line)
            away[g * span : (g + 1) * span] = jnp.concatenate(lines, axis=0).astype(bf16)
        where = slice(first * span, stop * span)
        for b in range(blocks):
            cols = slice(b * BLOCK, (b + 1) * BLOCK)
            deriv[where, cols] = deriv[where, cols] + jnp.dot(
                away[where], across_back[b], preferred_element_type=f32
            )

    def update(sec, first, count, at, b):
        start_part = (0.0, 0.75, 1.0 / 3.0)[sec]
        step_part = (1.0, 0.25, 2.0 / 3.0)[sec]
        for t in range(b * BLOCK // LANES, (b + 1) * BLOCK // LANES):
            cols = slice(t * LANES, (t + 1) * LANES)
            speed = jnp.broadcast_to(courant[:, cols], (heights, LANES))
            x = state[sec, pl.ds(first - HALO, count + 2 * HALO), :, cols]
            now = x[HALO : HALO + count]
            azimuth = None
            for o in range(1, 5):
                term = stencil_weights[o - 1] * (x[HALO + o : HALO + o + count] - x[HALO - o : HALO - o + count])
                azimuth = term if azimuth is None else azimuth + term
            slope = deriv[pl.ds(at, count * heights), cols].reshape(count, heights, LANES)
            moved = now - speed * azimuth - now * slope
            if sec > 0:
                moved = start_part * state[0, pl.ds(first, count), :, cols] + step_part * moved
            if sec < 2:
                state[sec + 1, pl.ds(first, count), :, cols] = moved
                keep_split(moved, at, cols)
            else:
                raw[t, pl.ds((first - HALO) * heights, count * heights)] = moved.reshape(-1, LANES)

    def emit(g):
        for t in range(tiles):
            for h in range(heights):
                out[pl.ds(pl.multiple_of(h * rows + g * GROUP, GROUP), GROUP), t * LANES : (t + 1) * LANES] = raw[
                    t, pl.ds(g * span + h, GROUP, stride=heights)
                ]

    for copy in loads:
        copy.wait()

    def stage(first, count, at):
        for t in range(tiles):
            cols = slice(t * LANES, (t + 1) * LANES)
            value = jnp.stack([raw[t, pl.ds(first - HALO + k, heights, stride=rows)] for k in range(count)])
            state[0, pl.ds(first, count), :, cols] = value
            keep_split(value, at, cols)

    stage(HALO, HALO, 0)
    stage(rows, HALO, HALO * heights)

    @pl.loop(1, groups)
    def _(g):
        stage(place(g), GROUP, pl.multiple_of(g * span, span))

    def inner(sec, part):
        far(sec, part)
        for b in range(blocks):
            for g in range(*parts[part]):
                update(sec, place(g), GROUP, g * span, b)
        if sec < 2:
            project(sec + 1, part)
            coefs(sec + 1, part).start()

    def edges(sec):
        far(sec, 0)
        for b in range(blocks):
            halo(sec, 0, b).wait_recv()
            halo(sec, 1, b).wait_recv()
            update(sec, HALO, HALO, 0, b)
            update(sec, rows, HALO, HALO * heights, b)
            if sec < 2:
                halo(sec + 1, 0, b).start()
                halo(sec + 1, 1, b).start()
        if sec < 2:
            project(sec + 1, 0)
            coefs(sec + 1, 0).start()

    for copy in tables:
        copy.wait()
    for part in (1, 2, 0):
        project(0, part)
    pl.semaphore_wait(barrier, 3)
    for part in (1, 2, 0):
        coefs(0, part).start()
    for b in range(blocks):
        halo(0, 0, b).start()
        halo(0, 1, b).start()

    for part in (1, 2, 0):
        near(part)
    for sec in range(2):
        inner(sec, 1)
        inner(sec, 2)
        near(1)
        edges(sec)
        near(2)
        near(0)
    inner(2, 1)
    inner(2, 2)

    @pl.loop(1, groups - 1)
    def _(g):
        emit(g)

    edges(2)
    emit(0)
    emit(groups - 1)

    for sec in range(3):
        for way in range(2):
            for b in range(blocks):
                halo(sec, way, b).wait_send()
        for part in range(len(parts)):
            coefs(sec, part).wait_send()


def body(size, field, courant):
    heights, rows, radial_count = field.shape
    tables = [jnp.asarray(t) for t in radial_tables(radial_count)]
    groups = rows // GROUP
    dma = pltpu.SemaphoreType.DMA
    anywhere = pl.BlockSpec(memory_space=pl.ANY)
    operands = [field, courant.reshape(1, -1)] + tables
    result = pl.pallas_call(
        functools.partial(kernel, size),
        out_shape=pltpu.VMEM((heights * rows, radial_count), f32),
        in_specs=[anywhere] * len(operands),
        out_specs=pl.BlockSpec(memory_space=pltpu.VMEM),
        scratch_shapes=[
            pltpu.VMEM((1, radial_count), f32),
            pltpu.VMEM(tables[0].shape, bf16),
            pltpu.VMEM((radial_count // BLOCK, 5 * BLOCK, BLOCK), bf16),
            pltpu.VMEM(tables[2].shape, bf16),
            pltpu.VMEM((radial_count // LANES, heights * rows, LANES), f32),
            pltpu.VMEM((3, rows + 2 * HALO, heights, radial_count), f32),
            pltpu.VMEM((rows * heights, radial_count), bf16),
            pltpu.VMEM((rows * heights, radial_count), bf16),
            pltpu.VMEM((rows * heights, LANES), bf16),
            pltpu.VMEM((rows * heights, 2 * LANES), bf16),
            pltpu.VMEM((rows * heights, radial_count), f32),
            pltpu.VMEM((3, groups, heights, LANES), f32),
            pltpu.VMEM((3, groups, heights, LANES), f32),
            dma((radial_count // LANES, heights)),
            dma((3 + len(fills),)),
            dma((3, 2, radial_count // BLOCK)),
            dma((3, 2, radial_count // BLOCK)),
            dma((3, 3)),
            dma((3, 3)),
        ],
        compiler_params=pltpu.CompilerParams(
            collective_id=0, has_side_effects=True, vmem_limit_bytes=40 << 20
        ),
    )(*[pltpu.with_memory_space_constraint(x, pltpu.HBM) for x in operands])
    return result.reshape(field.shape)


def solution(mesh):
    size = mesh.shape["theta"]
    return jax.shard_map(
        functools.partial(body, size),
        mesh=mesh,
        in_specs=(P("gz", "theta", None), P()),
        out_specs=P("gz", "theta", None),
        check_vma=False,
    )
```

```python
import functools
import math

import jax
import jax.numpy as jnp
import numpy as np
from jax import lax
from jax.experimental import pallas as pl
from jax.experimental.pallas import tpu as pltpu
from jax.sharding import PartitionSpec as P

stencil_weights = (4.0 / 5.0, -1.0 / 5.0, 4.0 / 105.0, -1.0 / 280.0)
radial_step = 0.2
BLOCK = 256
LANES = 128
FAR = 16
HALO = 4
GROUP = 8
MESH = pl.DeviceIdType.MESH
f32, bf16 = jnp.float32, jnp.bfloat16
fills = (
    (0, 0, BLOCK),
    (0, BLOCK, BLOCK),
    (BLOCK, 2 * BLOCK, BLOCK),
    (2 * BLOCK, 3 * BLOCK, LANES),
    (2 * BLOCK, 3 * BLOCK + LANES, LANES),
    (2 * BLOCK + LANES, 4 * BLOCK, LANES),
    (2 * BLOCK + LANES, 4 * BLOCK + LANES, LANES),
)


def best_shifts(delta, count):
    a, g, c = [1.0], [delta], [math.sqrt(1.0 - delta * delta)]
    for _ in range(9):
        a.append((a[-1] + g[-1]) / 2)
        c.append((a[-2] - g[-1]) / 2)
        g.append(math.sqrt(a[-2] * g[-1]))
    quarter = math.pi / (2 * a[-1])
    shifts = []
    for i in range(count):
        phi = 2 ** (len(a) - 1) * a[-1] * (2 * i + 1) * quarter / (2 * count)
        for k in range(len(a) - 1, 0, -1):
            phi = 0.5 * (phi + math.asin(max(-1.0, min(1.0, c[k] / a[k] * math.sin(phi)))))
        shifts.append(math.sqrt(math.cos(phi) ** 2 + (delta * math.sin(phi)) ** 2))
    return shifts


def rational_terms(points, shifts):
    columns, product = [], np.ones_like(points)
    for p in shifts:
        columns.append(math.sqrt(2 * p) / (points + p) * product)
        product = product * (points - p) / (points + p)
    return np.stack(columns, axis=1)


def rank_for(delta, tolerance):
    return math.ceil(math.log(4 / tolerance) * math.log(4 / delta) / math.pi**2)


def split_head(m):
    head = m.astype(np.float32).astype(bf16)
    tail = (m - head.astype(np.float64)).astype(np.float32).astype(bf16)
    return head, tail


def radial_tables(radial_count):
    last = 2 * radial_count - 1
    i = np.arange(radial_count)
    l = np.arange(last + 1)
    unit = np.pi / (2 * last)
    x = np.cos(2 * unit * i)
    gap = -2.0 * np.sin(unit * (i[:, None] + l)) * np.sin(unit * (i[:, None] - l))
    same = i[:, None] == l
    ci = np.where(i == 0, 2.0, 1.0)
    cl = np.where((l == 0) | (l == last), 2.0, 1.0)
    sign = np.where((i[:, None] + l) % 2 == 0, 1.0, -1.0)
    off = np.where(same, 0.0, ci[:, None] / cl * sign / np.where(same, 1.0, gap))
    near = (off - np.where(same, off.sum(axis=1)[:, None], 0.0))[:, :radial_count].T
    scale = radial_step / last * np.sin(2 * unit * i) ** 2
    blocks = radial_count // BLOCK
    diag = np.stack(
        [(near * scale)[b * BLOCK : (b + 1) * BLOCK, b * BLOCK : (b + 1) * BLOCK] for b in range(blocks)]
    )
    alternate = np.where(i % 2 == 0, 1.0, -1.0)
    row, column = alternate / ci, alternate * ci * scale
    into = np.zeros((radial_count, LANES))
    back = np.zeros((LANES, radial_count))
    at = 0
    for b in range(blocks):
        first, final = b * BLOCK, (b + 1) * BLOCK - 1
        low, high = x[final], x[first]
        above = x[first - 1] if b > 0 else x[-1]
        below = x[final + 1] if b < blocks - 1 else x[0]
        ratio = -((high - above) * (below - low)) / ((high - low) * (below - above))
        delta = ratio / (ratio + 2 + 2 * math.sqrt(ratio + 1))
        turn = (delta - 1) / (delta + 1) * (high - below) / (high - low)
        under = (x - below) - turn * (x - low)
        mapped = ((x - below) + turn * (x - low)) / under
        det = 2 * turn * (low - below)
        inside = (i >= first) & (i <= final)
        count = rank_for(delta, 1e-10)
        shifts = best_shifts(delta, count)
        into[inside, at : at + count] = rational_terms(mapped[inside], shifts) / under[inside, None]
        outer = rational_terms(-mapped[~inside], shifts) / under[~inside, None]
        back[at : at + count, ~inside] = (-det * outer).T
        at += count
    assert at <= LANES - FAR
    far = rational_terms(x, best_shifts(x[-1], FAR))
    into[:, LANES - FAR :] = far
    back[LANES - FAR :] = -far.T
    into *= row[:, None]
    back *= column
    diag_head, diag_tail = split_head(diag)
    into_parts = np.concatenate(split_head(into), axis=1)
    back_head, back_tail = split_head(back)
    back_head, back_tail = [m.reshape(LANES, blocks, BLOCK).transpose(1, 0, 2) for m in (back_head, back_tail)]
    both_parts = np.concatenate([diag_head, diag_tail, back_head, back_tail], axis=1)
    head, tail = back_head[:, LANES - FAR :], back_tail[:, LANES - FAR :]
    far_parts = np.concatenate([head, head, tail, tail], axis=1)
    far_parts = np.concatenate([far_parts, np.zeros((blocks, LANES - 4 * FAR, BLOCK), far_parts.dtype)], axis=1)
    return into_parts, both_parts, far_parts


def kernel(
    size,
    field,
    courant_in,
    into_in,
    both_in,
    across_in,
    out,
    courant,
    into,
    both,
    across_back,
    raw,
    state,
    head,
    tail,
    away,
    pair,
    deriv,
    packed,
    inbox,
    load_sem,
    table_sem,
    halo_send,
    halo_recv,
    coef_send,
    coef_recv,
):
    heights, rows, radial_count = field.shape
    blocks = radial_count // BLOCK
    groups = rows // GROUP
    span = GROUP * heights
    middle = groups // 2
    parts = ((0, 1), (1, middle), (middle, groups))
    tiles = radial_count // LANES
    me = lax.axis_index("theta")
    right = lax.rem(me + 1, size)
    left = lax.rem(me + size - 1, size)
    across = lax.rem(me + size // 2, size)

    barrier = pltpu.get_barrier_semaphore()
    for d in (right, left, across):
        pl.semaphore_signal(barrier, inc=1, device_id={"theta": d}, device_id_type=MESH)

    loads = [
        pltpu.make_async_copy(
            field.at[h, :, pl.ds(t * LANES, LANES)], raw.at[t, pl.ds(h * rows, rows)], load_sem.at[t, h]
        )
        for t in range(tiles)
        for h in range(heights)
    ]
    pairs = [(into_in, into), (courant_in, courant), (across_in, across_back)]
    for source, target, count in fills:
        pairs.append((both_in.at[:, pl.ds(source, count)], both.at[:, pl.ds(target, count)]))
    tables = [pltpu.make_async_copy(a, b, table_sem.at[k]) for k, (a, b) in enumerate(pairs)]
    for copy in loads + tables:
        copy.start()

    def halo(sec, way, b):
        if way == 0:
            source, target, device = HALO + rows - HALO, 0, right
        else:
            source, target, device = HALO, HALO + rows, left
        cols = pl.ds(b * BLOCK, BLOCK)
        return pltpu.make_async_remote_copy(
            state.at[sec, pl.ds(source, HALO), :, cols],
            state.at[sec, pl.ds(target, HALO), :, cols],
            halo_send.at[sec, way, b],
            halo_recv.at[sec, way, b],
            device_id={"theta": device},
            device_id_type=MESH,
        )

    def coefs(sec, part):
        first, stop = parts[part]
        where = pl.ds(first, stop - first)
        return pltpu.make_async_remote_copy(
            packed.at[sec, where],
            inbox.at[sec, where],
            coef_send.at[sec, part],
            coef_recv.at[sec, part],
            device_id={"theta": across},
            device_id_type=MESH,
        )

    def keep_split(value, at, cols):
        value = value.reshape(-1, value.shape[-1])
        top = value.astype(bf16)
        head[pl.ds(at, value.shape[0]), cols] = top
        tail[pl.ds(at, value.shape[0]), cols] = (value - top.astype(f32)).astype(bf16)

    def place(g):
        return HALO + HALO + (g - 1) * GROUP

    lane = lax.broadcasted_iota(jnp.int32, (heights, LANES), 1)

    def project(sec, part):
        first, stop = parts[part]
        where = slice(first * span, stop * span)
        for b in range(blocks):
            cols = slice(b * BLOCK, (b + 1) * BLOCK)
            line = jnp.concatenate([head[where, cols], tail[where, cols]], axis=1)
            deriv[where, cols] = jnp.dot(
                line, jnp.concatenate([into[cols], into[cols]], axis=0), preferred_element_type=f32
            )
        total = functools.reduce(
            lambda a, b: a + b, [deriv[where, k * LANES : (k + 1) * LANES] for k in range(radial_count // LANES)]
        )
        kept = jnp.where(lax.broadcasted_iota(jnp.int32, total.shape, 1) < LANES - FAR, total, 0.0)
        top = kept.astype(bf16)
        pair[where, 0:LANES] = top
        pair[where, LANES : 2 * LANES] = (kept - top.astype(f32)).astype(bf16)
        for g in range(first, stop):
            pack = jnp.zeros((heights, LANES), f32)
            for k in range(GROUP):
                r = (g - first) * span + k * heights
                moved = pltpu.roll(total[r : r + heights], (FAR * (k + 1)) % LANES, 1)
                pack = jnp.where((lane >= FAR * k) & (lane < FAR * (k + 1)), moved, pack)
            packed[sec, g] = pack

    def near(part):
        first, stop = parts[part]
        where = slice(first * span, stop * span)
        for b in range(blocks):
            cols = slice(b * BLOCK, (b + 1) * BLOCK)
            top = head[where, cols]
            wide = jnp.concatenate([top, tail[where, cols], top, pair[where], pair[where]], axis=1)
            deriv[where, cols] = jnp.dot(wide, both[b], preferred_element_type=f32)

    def far(sec, part):
        first, stop = parts[part]
        coefs(sec, part).wait_recv()
        for g in range(first, stop):
            pack = inbox[sec, g]
            top = pack.astype(bf16).astype(f32)
            rest = pack - top
            lines = []
            for k in range(GROUP):
                line = jnp.zeros((heights, LANES), f32)
                for n in range(4):
                    moved = pltpu.roll(rest if n % 2 else top, (FAR * (n - k)) % LANES, 1)
                    line = jnp.where((lane >= FAR * n) & (lane < FAR * (n + 1)), moved, line)
                lines.append(line)
            away[g * span : (g + 1) * span] = jnp.concatenate(lines, axis=0).astype(bf16)
        where = slice(first * span, stop * span)
        for b in range(blocks):
            cols = slice(b * BLOCK, (b + 1) * BLOCK)
            deriv[where, cols] = deriv[where, cols] + jnp.dot(
                away[where], across_back[b], preferred_element_type=f32
            )

    def update(sec, first, count, at, b):
        start_part = (0.0, 0.75, 1.0 / 3.0)[sec]
        step_part = (1.0, 0.25, 2.0 / 3.0)[sec]
        for t in range(b * BLOCK // LANES, (b + 1) * BLOCK // LANES):
            cols = slice(t * LANES, (t + 1) * LANES)
            speed = jnp.broadcast_to(courant[:, cols], (heights, LANES))
            x = state[sec, pl.ds(first - HALO, count + 2 * HALO), :, cols]
            now = x[HALO : HALO + count]
            azimuth = None
            for o in range(1, 5):
                term = stencil_weights[o - 1] * (x[HALO + o : HALO + o + count] - x[HALO - o : HALO - o + count])
                azimuth = term if azimuth is None else azimuth + term
            slope = deriv[pl.ds(at, count * heights), cols].reshape(count, heights, LANES)
            moved = now - speed * azimuth - now * slope
            if sec > 0:
                moved = start_part * state[0, pl.ds(first, count), :, cols] + step_part * moved
            if sec < 2:
                state[sec + 1, pl.ds(first, count), :, cols] = moved
                keep_split(moved, at, cols)
            else:
                raw[t, pl.ds((first - HALO) * heights, count * heights)] = moved.reshape(-1, LANES)

    def emit(g):
        for t in range(tiles):
            for h in range(heights):
                out[pl.ds(pl.multiple_of(h * rows + g * GROUP, GROUP), GROUP), t * LANES : (t + 1) * LANES] = raw[
                    t, pl.ds(g * span + h, GROUP, stride=heights)
                ]

    for copy in loads:
        copy.wait()

    def stage(first, count, at):
        for t in range(tiles):
            cols = slice(t * LANES, (t + 1) * LANES)
            value = jnp.stack([raw[t, pl.ds(first - HALO + k, heights, stride=rows)] for k in range(count)])
            state[0, pl.ds(first, count), :, cols] = value
            keep_split(value, at, cols)

    stage(HALO, HALO, 0)
    stage(rows, HALO, HALO * heights)

    @pl.loop(1, groups)
    def _(g):
        stage(place(g), GROUP, pl.multiple_of(g * span, span))

    def inner(sec, part):
        far(sec, part)
        for b in range(blocks):
            for g in range(*parts[part]):
                update(sec, place(g), GROUP, g * span, b)
        if sec < 2:
            project(sec + 1, part)
            coefs(sec + 1, part).start()

    def edges(sec):
        far(sec, 0)
        for b in range(blocks):
            halo(sec, 0, b).wait_recv()
            halo(sec, 1, b).wait_recv()
            update(sec, HALO, HALO, 0, b)
            update(sec, rows, HALO, HALO * heights, b)
            if sec < 2:
                halo(sec + 1, 0, b).start()
                halo(sec + 1, 1, b).start()
        if sec < 2:
            project(sec + 1, 0)
            coefs(sec + 1, 0).start()

    tables[0].wait()
    for part in (1, 2, 0):
        project(0, part)
    pl.semaphore_wait(barrier, 3)
    for part in (1, 2, 0):
        coefs(0, part).start()
    for b in range(blocks):
        halo(0, 0, b).start()
        halo(0, 1, b).start()

    for copy in tables[1:]:
        copy.wait()
    for part in (1, 2, 0):
        near(part)
    for sec in range(2):
        inner(sec, 1)
        inner(sec, 2)
        edges(sec)
        near(1)
        near(2)
        near(0)
    inner(2, 1)
    inner(2, 2)

    @pl.loop(1, groups - 1)
    def _(g):
        emit(g)

    edges(2)
    emit(0)
    emit(groups - 1)

    for sec in range(3):
        for way in range(2):
            for b in range(blocks):
                halo(sec, way, b).wait_send()
        for part in range(len(parts)):
            coefs(sec, part).wait_send()


def body(size, field, courant):
    heights, rows, radial_count = field.shape
    tables = [jnp.asarray(t) for t in radial_tables(radial_count)]
    groups = rows // GROUP
    dma = pltpu.SemaphoreType.DMA
    anywhere = pl.BlockSpec(memory_space=pl.ANY)
    operands = [field, courant.reshape(1, -1)] + tables
    result = pl.pallas_call(
        functools.partial(kernel, size),
        out_shape=pltpu.VMEM((heights * rows, radial_count), f32),
        in_specs=[anywhere] * len(operands),
        out_specs=pl.BlockSpec(memory_space=pltpu.VMEM),
        scratch_shapes=[
            pltpu.VMEM((1, radial_count), f32),
            pltpu.VMEM(tables[0].shape, bf16),
            pltpu.VMEM((radial_count // BLOCK, 5 * BLOCK, BLOCK), bf16),
            pltpu.VMEM(tables[2].shape, bf16),
            pltpu.VMEM((radial_count // LANES, heights * rows, LANES), f32),
            pltpu.VMEM((3, rows + 2 * HALO, heights, radial_count), f32),
            pltpu.VMEM((rows * heights, radial_count), bf16),
            pltpu.VMEM((rows * heights, radial_count), bf16),
            pltpu.VMEM((rows * heights, LANES), bf16),
            pltpu.VMEM((rows * heights, 2 * LANES), bf16),
            pltpu.VMEM((rows * heights, radial_count), f32),
            pltpu.VMEM((3, groups, heights, LANES), f32),
            pltpu.VMEM((3, groups, heights, LANES), f32),
            dma((radial_count // LANES, heights)),
            dma((3 + len(fills),)),
            dma((3, 2, radial_count // BLOCK)),
            dma((3, 2, radial_count // BLOCK)),
            dma((3, 3)),
            dma((3, 3)),
        ],
        compiler_params=pltpu.CompilerParams(
            collective_id=0, has_side_effects=True, vmem_limit_bytes=40 << 20
        ),
    )(*[pltpu.with_memory_space_constraint(x, pltpu.HBM) for x in operands])
    return result.reshape(field.shape)


def solution(mesh):
    size = mesh.shape["theta"]
    return jax.shard_map(
        functools.partial(body, size),
        mesh=mesh,
        in_specs=(P("gz", "theta", None), P()),
        out_specs=P("gz", "theta", None),
        check_vma=False,
    )
```
